512 devices in a mesh: seq: 32 (over z_lo, y, core), ch: 16 (over x, z_hi).
Axes of the slice: x: 4, y: 8, z: 8 (z_hi: 4, z_lo: 2; z = z_hi * 2 + z_lo), core: 2. Of those that a mesh axis runs over, the one named last changes fastest.
Arguments:
- tokens: bfloat16 [480, 65536], P('ch', 'seq'), may hold values from -6 to 6
- cotangent: bfloat16 [480, 65536], P('ch', 'seq'), may hold values from -6 to 6
- right_blocks: bfloat16 [16, 256, 256, 256], P('ch', 'seq'), may hold values from -0.375 to 0.375
- left_blocks: bfloat16 [16, 256, 256, 256], P('ch', 'seq'), may hold values from -0.375 to 0.375
- w_in: bfloat16 [480, 1920], P(None, 'ch'), may hold values from -0.25 to 0.25
- w_out: bfloat16 [1920, 480], P('ch'), may hold values from -0.125 to 0.125
Outputs:
- mixed: bfloat16 [480, 65536], P('ch', 'seq')
- grad_input: bfloat16 [480, 65536], P('ch', 'seq')
- grad_right: bfloat16 [16, 256, 256, 256], P('ch', 'seq')
- left_factor_gradient: bfloat16 [16, 256, 256, 256], P('ch', 'seq')
- grad_w_in: bfloat16 [480, 1920], P(None, 'ch')
- grad_w_out: bfloat16 [1920, 480], P('ch')
The draws below stay inside these ranges and needn't reach their ends.
All inputs are finite; a program needn't handle non-finite values.
Results may differ from the reference program's by a relative error of at most 0.03.
Values may be sent and summed in bfloat16 or wider, within the bound.
A program may use at most 64 MiB of HBM per device.

```python
import jax
import jax.numpy as jnp
from jax import lax

D = 480
FF = 1920
BLK = 256
SEQ_BLOCKS = 256
TOKENS = 65536
GROUPS = 16
GROUP_CH = 30
HID_DEV = 120


def shard_levels(key, extent, pieces, smallest, top_value):
    level = 1.0
    for axis_at, parts in pieces:
        steps = jax.random.uniform(jax.random.fold_in(jax.random.fold_in(key, 6), axis_at), (parts,), jnp.float32, smallest / len(pieces), top_value / len(pieces))
        level = level * jnp.repeat(jnp.exp(steps), extent[axis_at] // parts).reshape((-1,) + (1,) * (len(extent) - 1 - axis_at))
    return level


def gaussian(own_key, shape, deviation, limit, cuts=(), kind=jnp.bfloat16):
    array = jax.random.normal(own_key, shape, jnp.float32) * deviation
    if len(cuts) > 0:
        array = shard_levels(own_key, shape, cuts, -0.22, 0.18) * array
    return jnp.clip(array, min=-limit, max=limit).astype(kind)


def setup_inputs(seed: int = 0) -> dict:
    seeds = jax.random.split(jax.random.key(seed), 7)
    tokens = gaussian(seeds[0], (D, TOKENS), 1.0, 6.0, ((0, 16), (1, 32)))
    cotangent = gaussian(seeds[1], (D, TOKENS), 1.0, 6.0, ((0, 16), (1, 32)))
    right_blocks = gaussian(seeds[2], (GROUPS, SEQ_BLOCKS, BLK, BLK), BLK ** -0.5, 0.375, ((0, 16), (1, 32)))
    left_blocks = gaussian(seeds[3], (GROUPS, BLK, SEQ_BLOCKS, SEQ_BLOCKS), SEQ_BLOCKS ** -0.5, 0.375, ((0, 16), (1, 32)))
    w_in = gaussian(seeds[4], (D, FF), D ** -0.5, 0.25, ((1, 16),))
    w_out = gaussian(seeds[5], (FF, D), FF ** -0.5, 0.125, ((0, 16),))
    return dict(tokens=tokens, cotangent=cotangent, right_blocks=right_blocks, left_blocks=left_blocks, w_in=w_in, w_out=w_out)


def gelu_value(value_in):
    return 0.5 * value_in * (1.0 + lax.erf(value_in * 0.7071067811865476))


def gelu_slope(value_in):
    return 0.5 * (1.0 + lax.erf(value_in * 0.7071067811865476)) + value_in * jnp.exp(-0.5 * value_in * value_in) * 0.3989422804014327


def forward_group(group_args):
    token_blocks, right_group, left_factor_group = group_args
    block_layout = jnp.einsum("ikj,cij->cik", right_group.astype(jnp.float32), token_blocks.astype(jnp.float32)).astype(jnp.bfloat16)
    monarch_product = jnp.einsum("ewm,qme->qwe", left_factor_group.astype(jnp.float32), block_layout.astype(jnp.float32)).astype(jnp.bfloat16)
    return block_layout, monarch_product


def backward_group(group_args):
    monarch_product_gradient, block_layout, token_blocks, right_group, left_factor_group = group_args
    left_factor_gradient = jnp.einsum("aty,ahy->yth", monarch_product_gradient.astype(jnp.float32), block_layout.astype(jnp.float32)).astype(jnp.bfloat16)
    block_layout_gradient = jnp.einsum("jys,dyj->dsj", left_factor_group.astype(jnp.float32), monarch_product_gradient.astype(jnp.float32)).astype(jnp.bfloat16)
    grad_right = jnp.einsum("cik,cij->ikj", block_layout_gradient.astype(jnp.float32), token_blocks.astype(jnp.float32)).astype(jnp.bfloat16)
    from_right = jnp.einsum("ikj,cik->cij", right_group.astype(jnp.float32), block_layout_gradient.astype(jnp.float32))
    return left_factor_gradient, grad_right, from_right


def reference(tokens, cotangent, right_blocks, left_blocks, w_in, w_out):
    token_groups = tokens.reshape(GROUPS, GROUP_CH, SEQ_BLOCKS, BLK)
    block_layout, monarch_product = lax.map(forward_group, (token_groups, right_blocks, left_blocks))
    monarch_f = monarch_product.reshape(D, TOKENS).astype(jnp.float32)
    tokens_f = tokens.astype(jnp.float32)
    sigma = jax.nn.sigmoid(tokens_f)
    silu_x = tokens_f * sigma
    slope_silu = sigma * (1.0 + tokens_f * (1.0 - sigma))
    gate_out = (tokens_f + monarch_f * silu_x).astype(jnp.bfloat16)

    gate_blocks = jnp.moveaxis(gate_out.reshape(D, SEQ_BLOCKS, BLK), 1, 0)
    cot_blocks = jnp.moveaxis(cotangent.reshape(D, SEQ_BLOCKS, BLK), 1, 0)
    w_out_groups = w_out.astype(jnp.float32).reshape(GROUPS, HID_DEV, D)
    w_in_groups = w_in.astype(jnp.float32).reshape(D, GROUPS, HID_DEV)

    def mlp_block(carry, block_args):
        grad_in_sum, grad_out_sum = carry
        gate_block, cot_block = block_args
        pre_act = jnp.dot(w_in.T, gate_block, preferred_element_type=jnp.float32)
        hidden = gelu_value(pre_act).astype(jnp.bfloat16)
        partials = jnp.einsum("ghd,ght->gdt", w_out_groups, hidden.astype(jnp.float32).reshape(GROUPS, HID_DEV, BLK))
        mlp_out = jnp.sum(partials.astype(jnp.bfloat16).astype(jnp.float32), axis=0)
        mixed_block = (gate_block.astype(jnp.float32) + mlp_out).astype(jnp.bfloat16)
        back_grad = jnp.dot(w_out, cot_block, preferred_element_type=jnp.float32)
        pre_grad = (back_grad * gelu_slope(pre_act)).astype(jnp.bfloat16)
        back_parts = jnp.einsum("dgh,ght->gdt", w_in_groups, pre_grad.astype(jnp.float32).reshape(GROUPS, HID_DEV, BLK))
        up_sum = jnp.sum(back_parts.astype(jnp.bfloat16).astype(jnp.float32), axis=0)
        grad_in_sum = grad_in_sum + jnp.dot(gate_block, pre_grad.T, preferred_element_type=jnp.float32)
        grad_out_sum = grad_out_sum + jnp.dot(hidden, cot_block.T, preferred_element_type=jnp.float32)
        return (grad_in_sum, grad_out_sum), (mixed_block, up_sum)

    start_carry = (jnp.zeros((D, FF), jnp.float32), jnp.zeros((FF, D), jnp.float32))
    (grad_in_sum, grad_out_sum), (mixed_blocks, up_sums) = lax.scan(mlp_block, start_carry, (gate_blocks, cot_blocks))
    mixed = jnp.moveaxis(mixed_blocks, 0, 1).reshape(D, TOKENS)
    gate_grad = cotangent.astype(jnp.float32) + jnp.moveaxis(up_sums, 0, 1).reshape(D, TOKENS)
    monarch_product_gradient = (gate_grad * silu_x).astype(jnp.bfloat16).reshape(GROUPS, GROUP_CH, SEQ_BLOCKS, BLK)
    left_factor_gradient, grad_right, from_right = lax.map(backward_group, (monarch_product_gradient, block_layout, token_groups, right_blocks, left_blocks))
    grad_input = (gate_grad * (1.0 + monarch_f * slope_silu) + from_right.reshape(D, TOKENS)).astype(jnp.bfloat16)
    return (mixed, grad_input, grad_right, left_factor_gradient, grad_in_sum.astype(jnp.bfloat16), grad_out_sum.astype(jnp.bfloat16))
```

```python
import jax
import jax.numpy as jnp
from jax import lax
from jax.experimental import pallas as pl
from jax.experimental.pallas import tpu as pltpu
from jax.sharding import PartitionSpec as P

NS = 32
NC = 16
GC = 30
HID = 120
F32 = jnp.float32
BF16 = jnp.bfloat16
MESH = pl.DeviceIdType.MESH

NN = (((1,), (0,)), ((), ()))
NT = (((1,), (1,)), ((), ()))
TN = (((0,), (0,)), ((), ()))

A1, A2, A3, A4, XC, WT, XG, XU, XM, GX, GS, GA = range(12)


def dot(a, b, dims=NN):
    return lax.dot_general(a, b, dims, preferred_element_type=F32)


def one_hot(shape, test):
    rows = lax.broadcasted_iota(jnp.int32, shape, 0)
    cols = lax.broadcasted_iota(jnp.int32, shape, 1)
    return jnp.where(test(rows, cols), 1.0, 0.0).astype(BF16)


def gelu_parts(v):
    cdf = 0.5 * (1.0 + lax.erf(v * 0.7071067811865476))
    return v * cdf, cdf + v * jnp.exp(-0.5 * v * v) * 0.3989422804014327


def kernel(
    tok_h, cot_h, r_h, l_h, wi_h, wo_h,
    mixed_h, gin_h, gr_h, gl_h, gwi_h, gwo_h,
    tok_v, cot_v, r_v, l_v, wi_v, wo_v,
    tokp, cots, s1, r1, s2, r2, s3, r3, s4, r4,
    fold_src, ct, mon, go, gf, cf, ws, w12, w1t, w2t, back, hid, pg,
    su, ru, sm, rm, sg, rg, sh, rh, sf, rf, gg,
    mixed_v, gin_v, gl_v, gr_v, gwi_v, gwo_v,
    in_sem, out_sem, send_sem, recv_sem,
):
    s, c = lax.axis_index("seq"), lax.axis_index("ch")
    cx, cz = c // 4, lax.rem(c, 4)

    barrier = pltpu.get_barrier_semaphore()

    @pl.loop(1, NS)
    def _(o):
        pl.semaphore_signal(barrier, inc=1, device_id={"seq": lax.rem(s + o, NS), "ch": c}, device_id_type=MESH)

    @pl.loop(1, NC)
    def _(o):
        pl.semaphore_signal(barrier, inc=1, device_id={"seq": s, "ch": lax.rem(c + o, NC)}, device_id_type=MESH)

    ins = [
        pltpu.make_async_copy(src, dst, in_sem.at[n])
        for n, (src, dst) in enumerate(
            ((tok_h, tok_v), (r_h, r_v), (cot_h, cot_v), (wi_h, wi_v), (wo_h, wo_v), (l_h, l_v))
        )
    ]
    for copy in ins:
        copy.start()

    def send(which, src, dst, seq, ch):
        pltpu.make_async_remote_copy(
            src_ref=src, dst_ref=dst, send_sem=send_sem.at[which], recv_sem=recv_sem.at[which],
            device_id={"seq": seq, "ch": ch}, device_id_type=MESH,
        ).start()

    def over_seq(which, src_of, dst):
        @pl.loop(1, NS)
        def _(o):
            t = lax.rem(s + o, NS)
            send(which, src_of(t), dst.at[s], t, c)

    def arrived(which, view):
        pltpu.make_async_copy(view, view, recv_sem.at[which]).wait()

    def sent(which, view):
        pltpu.make_async_copy(view, view, send_sem.at[which]).wait()

    eye = one_hot((256, 256), lambda a, b: a == b)
    fold_t = one_hot((32, 256), lambda a, b: a == (b & 31))
    keep = (
        (lax.broadcasted_iota(jnp.int32, (8, 256), 1) >> 5) == lax.broadcasted_iota(jnp.int32, (8, 256), 0)
    )[None]

    def spread(n):
        row = jnp.broadcast_to(fold_src[:, n : n + 1, :], (NS, 8, 256))
        return jnp.where(keep, row, 0.0).reshape(256, 256).astype(BF16)

    def flip(rows, dst):
        stacked = jnp.concatenate([row.astype(BF16) for row in rows], axis=0)
        dst[...] = dot(eye, stacked, NT).reshape(NS, 8, 256).astype(BF16)

    ins[0].wait()
    tokp[...] = jnp.zeros_like(tokp)
    for i in range(8):
        tokp[i, 0:GC, :] = tok_v[:, 256 * i : 256 * i + 256]
    ins[1].wait()
    flip([dot(tokp[i], r_v[i], NT) for i in range(8)], s1)
    r1[s] = s1[s]

    ins[2].wait()
    cots[...] = jnp.zeros_like(cots)
    for q in range(4):
        cots[q, 0:GC, :] = cot_v[:, 512 * q : 512 * q + 512]
    cf[c] = cots[cx]
    pad_cols = one_hot(
        (GC * NC, 512), lambda a, b: (a == GC * (b >> 5) + (b & 31)) & ((b & 31) < GC)
    )
    ins[3].wait()
    ins[4].wait()
    ws[...] = jnp.zeros_like(ws)
    ws[0, 0:HID, :] = dot(wi_v[...], pad_cols, TN).astype(BF16)
    ws[1, 0:HID, :] = dot(wo_v[...], pad_cols).astype(BF16)
    w12[cx] = ws[...]

    pl.semaphore_wait(barrier, NS + NC - 2)
    over_seq(A1, lambda t: s1.at[t], r1)

    @pl.loop(1, NC)
    def _(o):
        t = lax.rem(c + o, NC)
        send(XC, cots.at[t // 4], cf.at[c], s, t)

    @pl.loop(1, 4)
    def _(o):
        t = lax.rem(cx + o, 4) * 4 + cz
        send(WT, ws, w12.at[cx], s, t)

    ins[5].wait()
    arrived(A1, r1.at[pl.ds(0, NS - 1)])
    fold_src[...] = r1[...].astype(F32)
    for k in range(8):
        ct[k] = dot(fold_t, spread(k), NT).astype(BF16)
    flip([dot(ct[k], l_v[k], NT) for k in range(8)], s2)
    r2[s] = s2[s]
    over_seq(A2, lambda t: s2.at[t], r2)

    arrived(WT, w12.at[pl.ds(0, 3)])
    eye128 = one_hot((128, 128), lambda a, b: a == b)
    for b in range(4):
        for h in range(4):
            cols = slice(128 * b, 128 * b + 128)
            w1t[b, :, 128 * h : 128 * h + 128] = dot(eye128, w12[h, 0, :, cols], NT).astype(BF16)
            w2t[b, :, 128 * h : 128 * h + 128] = dot(eye128, w12[h, 1, :, cols], NT).astype(BF16)
    arrived(XC, cf.at[pl.ds(0, NC - 1)])
    cot_all = cf[...].reshape(512, 512)
    for h in range(4):
        back[h] = dot(w12[h, 1], cot_all)

    arrived(A2, r2.at[pl.ds(0, NS - 1)])
    fold_src[...] = r2[...].astype(F32)
    for l in range(8):
        m = dot(fold_t, spread(l), NT)
        mon[l] = m
        t = tokp[l].astype(F32)
        go[l // 2, :, 256 * (l % 2) : 256 * (l % 2) + 256] = (t + m * (t * jax.nn.sigmoid(t))).astype(BF16)
    gf[c] = go[cx]

    @pl.loop(1, NC)
    def _(o):
        t = lax.rem(c + o, NC)
        send(XG, go.at[t // 4], gf.at[c], s, t)

    arrived(XG, gf.at[pl.ds(0, NC - 1)])
    gate_all = gf[...].reshape(512, 512)
    for h in range(4):
        value, slope = gelu_parts(dot(w12[h, 0], gate_all))
        hid[h] = value.astype(BF16)
        pg[h] = (back[h] * slope).astype(BF16)

    def partials(which, weights, units, dst, remote):
        all_units = units[...].reshape(512, 512)
        for j in range(4):
            b = lax.rem(cx + j, 4)
            dst[pl.ds(4 * b, 4)] = dot(weights[b], all_units).reshape(4, 32, 512).astype(BF16)
            for m in range(4):
                t = 4 * b + lax.rem(cz + m, 4)
                if j == 0 and m == 0:
                    continue
                send(which, dst.at[t], remote.at[c], s, t)
        remote[c] = dst[c]

    partials(XU, w1t, pg, su, ru)

    for h in range(4):
        sg[h, 0] = dot(pg[h], gate_all, NT).astype(BF16)
        sg[h, 1] = dot(hid[h], cot_all, NT).astype(BF16)
    rg[cx] = sg[cx]

    @pl.loop(1, 4)
    def _(o):
        x = lax.rem(cx + o, 4)
        send(GX, sg.at[x], rg.at[cx], s, x * 4 + cz)

    partials(XM, w2t, hid, sm, rm)

    arrived(XU, ru.at[pl.ds(0, NC - 1)])

    def summed(parts, l):
        q, at = l // 2, slice(256 * (l % 2), 256 * (l % 2) + 256)
        total = parts[4 * q, :, at].astype(F32)
        for z in range(1, 4):
            total = total + parts[4 * q + z, :, at].astype(F32)
        return total

    rows = []
    for l in range(8):
        t = tokp[l].astype(F32)
        g = cots[l // 2, :, 256 * (l % 2) : 256 * (l % 2) + 256].astype(F32) + summed(ru, l)
        gg[l] = g
        rows.append(g * (t * jax.nn.sigmoid(t)))
    flip(rows, s3)
    r3[s] = s3[s]
    over_seq(A3, lambda t: s3.at[t], r3)

    arrived(GX, rg.at[pl.ds(0, 3)])
    for n in range(2):
        total = rg[0, n].astype(F32)
        for x in range(1, 4):
            total = total + rg[x, n].astype(F32)
        sh[16 * n : 16 * n + 16] = total.reshape(16, 8, 512).astype(BF16)
    rh[s] = sh[s]
    over_seq(GS, lambda t: sh.at[t], rh)

    arrived(A3, r3.at[pl.ds(0, NS - 1)])
    fold_src[...] = r3[...].astype(F32)
    flip([dot(dot(fold_t, spread(k), NT).astype(BF16), l_v[k]) for k in range(8)], s4)
    r4[s] = s4[s]
    over_seq(A4, lambda t: s4.at[t], r4)

    arrived(GS, rh.at[pl.ds(0, NS - 1)])
    sf[...] = jnp.sum(rh[...].astype(F32), axis=0).astype(BF16)
    rf[s] = sf[...]
    over_seq(GA, lambda t: sf, rf)

    for k in range(8):
        g = dot(spread(k), fold_t, NT).astype(BF16)
        gl_v[k] = dot(g, ct[k]).astype(BF16)

    arrived(XM, rm.at[pl.ds(0, NC - 1)])
    for l in range(8):
        at = slice(256 * (l % 2), 256 * (l % 2) + 256)
        value = (go[l // 2, :, at].astype(F32) + summed(rm, l)).astype(BF16)
        mixed_v[:, 256 * l : 256 * l + 256] = value[0:GC]
    outs = [pltpu.make_async_copy(gl_v, gl_h, out_sem.at[0]), pltpu.make_async_copy(mixed_v, mixed_h, out_sem.at[1])]
    for copy in outs:
        copy.start()

    arrived(A4, r4.at[pl.ds(0, NS - 1)])
    fold_src[...] = r4[...].astype(F32)
    for i in range(8):
        x = spread(i)
        g = dot(x, fold_t, NT).astype(BF16)
        g_t = dot(fold_t, x, NT).astype(BF16)
        gr_v[i] = dot(g, tokp[i]).astype(BF16)
        t = tokp[i].astype(F32)
        sigma = jax.nn.sigmoid(t)
        through = gg[i] * (1.0 + mon[i] * (sigma * (1.0 + t * (1.0 - sigma))))
        value = (through + dot(g_t, r_v[i])).astype(BF16)
        gin_v[:, 256 * i : 256 * i + 256] = value[0:GC]
    outs += [pltpu.make_async_copy(gr_v, gr_h, out_sem.at[2]), pltpu.make_async_copy(gin_v, gin_h, out_sem.at[3])]
    for copy in outs[2:]:
        copy.start()

    arrived(GA, rf.at[pl.ds(0, NS - 1)])
    gwi_v[...] = dot(pad_cols, rf[0:16].reshape(128, 512), NT)[:, 0:HID].astype(BF16)
    gwo_v[...] = dot(rf[16:32].reshape(128, 512), pad_cols, NT)[0:HID].astype(BF16)
    outs += [pltpu.make_async_copy(gwi_v, gwi_h, out_sem.at[4]), pltpu.make_async_copy(gwo_v, gwo_h, out_sem.at[5])]
    for copy in outs[4:]:
        copy.start()

    for which, view in (
        (A1, s1.at[pl.ds(0, NS - 1)]), (A2, s2.at[pl.ds(0, NS - 1)]), (A3, s3.at[pl.ds(0, NS - 1)]),
        (A4, s4.at[pl.ds(0, NS - 1)]), (XC, cf.at[pl.ds(0, NC - 1)]), (WT, w12.at[pl.ds(0, 3)]),
        (XG, gf.at[pl.ds(0, NC - 1)]), (XU, su.at[pl.ds(0, NC - 1)]),
        (XM, sm.at[pl.ds(0, NC - 1)]), (GX, sg.at[pl.ds(0, 3)]), (GS, sh.at[pl.ds(0, NS - 1)]),
        (GA, rf.at[pl.ds(0, NS - 1)]),
    ):
        sent(which, view)
    for copy in outs:
        copy.wait()


def local(tokens, cotangent, right_blocks, left_blocks, w_in, w_out):
    piece = (NS, 8, 256)
    scratch = [
        ((GC, 2048), BF16), ((GC, 2048), BF16), ((8, 256, 256), BF16), ((8, 256, 256), BF16),
        ((480, HID), BF16), ((HID, 480), BF16),
        ((8, 32, 256), BF16), ((4, 32, 512), BF16),
        (piece, BF16), (piece, BF16), (piece, BF16), (piece, BF16),
        (piece, BF16), (piece, BF16), (piece, BF16), (piece, BF16),
        (piece, F32), ((8, 32, 256), BF16), ((8, 32, 256), F32),
        ((4, 32, 512), BF16), ((16, 32, 512), BF16), ((16, 32, 512), BF16),
        ((2, 128, 512), BF16), ((4, 2, 128, 512), BF16),
        ((4, 128, 512), BF16), ((4, 128, 512), BF16), ((4, 128, 512), F32),
        ((4, 128, 512), BF16), ((4, 128, 512), BF16),
        ((16, 32, 512), BF16), ((16, 32, 512), BF16), ((16, 32, 512), BF16), ((16, 32, 512), BF16),
        ((4, 2, 128, 512), BF16), ((4, 2, 128, 512), BF16),
        ((NS, 8, 512), BF16), ((NS, 8, 512), BF16), ((8, 512), BF16), ((NS, 8, 512), BF16),
        ((8, 32, 256), F32),
        ((GC, 2048), BF16), ((GC, 2048), BF16), ((8, 256, 256), BF16), ((8, 256, 256), BF16),
        ((480, HID), BF16), ((HID, 480), BF16),
    ]
    shapes = [
        ((GC, 2048), BF16), ((GC, 2048), BF16), ((8, 256, 256), BF16), ((8, 256, 256), BF16),
        ((480, HID), BF16), ((HID, 480), BF16),
    ]
    mixed, gin, gr, gl, gwi, gwo = pl.pallas_call(
        kernel,
        out_shape=[jax.ShapeDtypeStruct(*shape) for shape in shapes],
        in_specs=[pl.BlockSpec(memory_space=pl.ANY)] * 6,
        out_specs=[pl.BlockSpec(memory_space=pl.ANY)] * 6,
        scratch_shapes=[pltpu.VMEM(*shape) for shape in scratch]
        + [pltpu.SemaphoreType.DMA((6,)), pltpu.SemaphoreType.DMA((6,))]
        + [pltpu.SemaphoreType.DMA((12,)), pltpu.SemaphoreType.DMA((12,))],
        compiler_params=pltpu.CompilerParams(
            collective_id=0, has_side_effects=True, vmem_limit_bytes=48 * 1024 * 1024
        ),
        name="monarch_block",
    )(tokens, cotangent, right_blocks[0], left_blocks[0], w_in, w_out)
    return mixed, gin, gr[None], gl[None], gwi, gwo


def solution(mesh):
    placed = (
        P("ch", "seq"),
        P("ch", "seq"),
        P("ch", "seq", None, None),
        P("ch", "seq", None, None),
        P(None, "ch"),
        P("ch", None),
    )
    return jax.shard_map(
        local,
        mesh=mesh,
        in_specs=placed,
        out_specs=placed,
        check_vma=False,
    )
```

```python
import jax
import jax.numpy as jnp
from jax import lax
from jax.experimental import pallas as pl
from jax.experimental.pallas import tpu as pltpu
from jax.sharding import PartitionSpec as P

NS = 32
NC = 16
GC = 30
HID = 120
VMEM_LIMIT = 60 * 1024 * 1024
F32 = jnp.float32
BF16 = jnp.bfloat16
MESH = pl.DeviceIdType.MESH

NN = (((1,), (0,)), ((), ()))
NT = (((1,), (1,)), ((), ()))
TN = (((0,), (0,)), ((), ()))

A1, A2, A3, A4 = 0, 1, 2, 3
C1, C2, G1, G2 = 4, 8, 9, 13
WZ, WC = 14, 15
U1, U2, M1, M2 = 16, 20, 21, 22
PC, PZ, PS, PA = 23, 24, 25, 26
N_SEM = 27


def dot(a, b, dims=NN):
    return lax.dot_general(a, b, dims, preferred_element_type=F32)


def one_hot(shape, test):
    rows = lax.broadcasted_iota(jnp.int32, shape, 0)
    cols = lax.broadcasted_iota(jnp.int32, shape, 1)
    return jnp.where(test(rows, cols), 1.0, 0.0).astype(BF16)


def gelu_parts(v):
    cdf = 0.5 * (1.0 + lax.erf(v * 0.7071067811865476))
    return v * cdf, cdf + v * jnp.exp(-0.5 * v * v) * 0.3989422804014327


def kernel(
    tok_h, cot_h, r_h, l_h, wi_h, wo_h,
    mixed_h, gin_h, gr_h, gl_h, gwi_h, gwo_h,
    tok_v, cot_v, r_v, l_v, wi_v, wo_v,
    tokp, cots, s1, r1, s2, r2, s3, r3, s4, r4,
    fold_src, ct, mon, go, gf, cf, ws, w12, w1t, w2t, back, hid, pg,
    su, ru, su2, ru2, sm, rm, sm2, rm2,
    sg, sx, sp, rp, sh, rh, sf, rf, gg,
    mixed_v, gin_v, gl_v, gr_v, gwi_v, gwo_v,
    in_sem, out_sem, send_sem, recv_sem,
):
    s, c = lax.axis_index("seq"), lax.axis_index("ch")
    cx, cz = c // 4, lax.rem(c, 4)
    core = lax.rem(s, 2)
    pair = s // 2
    other = s + 1 - 2 * core

    barrier = pltpu.get_barrier_semaphore()

    @pl.loop(1, NS)
    def _(o):
        pl.semaphore_signal(barrier, inc=1, device_id={"seq": lax.rem(s + o, NS), "ch": c}, device_id_type=MESH)

    @pl.loop(1, NC)
    def _(o):
        pl.semaphore_signal(barrier, inc=1, device_id={"seq": s, "ch": lax.rem(c + o, NC)}, device_id_type=MESH)

    ins = [
        pltpu.make_async_copy(src, dst, in_sem.at[n])
        for n, (src, dst) in enumerate(
            ((tok_h, tok_v), (r_h, r_v), (cot_h, cot_v), (wi_h, wi_v), (wo_h, wo_v), (l_h, l_v))
        )
    ]
    for copy in ins:
        copy.start()

    pending = []

    def send(which, src, dst, seq, ch):
        pltpu.make_async_remote_copy(
            src_ref=src, dst_ref=dst, send_sem=send_sem.at[which], recv_sem=recv_sem.at[which],
            device_id={"seq": seq, "ch": ch}, device_id_type=MESH,
        ).start()

    def over_seq(which, src_of, dst):
        @pl.loop(1, NS)
        def _(o):
            t = lax.rem(s + o, NS)
            send(which, src_of(t), dst.at[s], t, c)

        pending.append((which, dst.at[pl.ds(0, NS - 1)]))

    def along_x(which, src, dst):
        for o in (1, 2, 3):
            send(which, src, dst, s, lax.rem(cx + o, 4) * 4 + cz)

    def along_z(o):
        return lax.rem(cz + o, 4), lax.rem(cz + 4 - o, 4)

    def arrived(which, view):
        pltpu.make_async_copy(view, view, recv_sem.at[which]).wait()

    def sent(which, view):
        pltpu.make_async_copy(view, view, send_sem.at[which]).wait()

    def gather_first(z_sem, x_sem, src, dst):
        for o in (2, 1, 3):
            to, _ = along_z(o)
            send(z_sem + o, src.at[to], dst.at[c], s, 4 * cx + to)
            pending.append((z_sem + o, dst.at[0]))
        dst[c] = src[cz]
        along_x(x_sem, src.at[cz], dst.at[c])

    def gather_second(z_sem, x_sem, dst):
        for o in (1, 3, 2):
            _, frm = along_z(o)
            arrived(z_sem + o, dst.at[0])
            along_x(x_sem, dst.at[4 * cx + frm], dst.at[4 * cx + frm])
        pending.append((x_sem, dst.at[pl.ds(0, 12)]))

    eye = one_hot((256, 256), lambda a, b: a == b)
    fold_t = one_hot((32, 256), lambda a, b: a == (b & 31))
    keep = (
        (lax.broadcasted_iota(jnp.int32, (8, 256), 1) >> 5) == lax.broadcasted_iota(jnp.int32, (8, 256), 0)
    )[None]

    def spread(n):
        row = jnp.broadcast_to(fold_src[:, n : n + 1, :], (NS, 8, 256))
        return jnp.where(keep, row, 0.0).reshape(256, 256).astype(BF16)

    def flip(rows, dst):
        stacked = jnp.concatenate([row.astype(BF16) for row in rows], axis=0)
        dst[...] = dot(eye, stacked, NT).reshape(NS, 8, 256).astype(BF16)

    ins[0].wait()
    tokp[...] = jnp.zeros_like(tokp)
    for i in range(8):
        tokp[i, 0:GC, :] = tok_v[:, 256 * i : 256 * i + 256]
    ins[1].wait()
    flip([dot(tokp[i], r_v[i], NT) for i in range(8)], s1)
    r1[s] = s1[s]
    pl.semaphore_wait(barrier, NS + NC - 2)
    over_seq(A1, lambda t: s1.at[t], r1)

    ins[2].wait()
    cots[...] = jnp.zeros_like(cots)
    for q in range(4):
        cots[q, 0:GC, :] = cot_v[:, 512 * q : 512 * q + 512]
    gather_first(C1, C2, cots, cf)
    pad_cols = one_hot(
        (GC * NC, 512), lambda a, b: (a == GC * (b >> 5) + (b & 31)) & ((b & 31) < GC)
    )
    ins[3].wait()
    ins[4].wait()
    for n, rows in enumerate((dot(wi_v[...], pad_cols, TN), dot(wo_v[...], pad_cols))):
        ws[0, n] = rows[0:64].astype(BF16)
        ws[1, n] = jnp.zeros((64, 512), BF16)
        ws[1, n, 0 : HID - 64, :] = rows[64:HID].astype(BF16)
    w12[core, cz] = ws[core]
    for o in (1, 2, 3):
        to, _ = along_z(o)
        send(WZ, ws.at[core], w12.at[core, cz], s, 4 * cx + to)
    pending.append((WZ, w12.at[0, pl.ds(0, 3)]))

    ins[5].wait()
    arrived(A1, r1.at[pl.ds(0, NS - 1)])
    fold_src[...] = r1[...].astype(F32)
    for k in range(8):
        ct[k] = dot(fold_t, spread(k), NT).astype(BF16)
    flip([dot(ct[k], l_v[k], NT) for k in range(8)], s2)
    r2[s] = s2[s]
    over_seq(A2, lambda t: s2.at[t], r2)
    gather_second(C1, C2, cf)

    arrived(A2, r2.at[pl.ds(0, NS - 1)])
    fold_src[...] = r2[...].astype(F32)
    for l in range(8):
        m = dot(fold_t, spread(l), NT)
        mon[l] = m
        t = tokp[l].astype(F32)
        go[l // 2, :, 256 * (l % 2) : 256 * (l % 2) + 256] = (t + m * (t * jax.nn.sigmoid(t))).astype(BF16)
    gather_first(G1, G2, go, gf)
    arrived(WZ, w12.at[0, pl.ds(0, 3)])
    send(WC, w12.at[core], w12.at[core], other, c)
    pending.append((WC, w12.at[0]))
    gather_second(G1, G2, gf)

    arrived(WC, w12.at[0])
    eye128 = one_hot((128, 128), lambda a, b: a == b)

    def weight(h, n):
        return w12[:, h, n].reshape(128, 512)

    for h in range(4):
        for n, turned in enumerate((w1t, w2t)):
            held = weight(h, n)
            for b in range(4):
                turned[b, :, 128 * h : 128 * h + 128] = dot(
                    eye128, held[:, 128 * b : 128 * b + 128], NT
                ).astype(BF16)
    arrived(C2, cf.at[pl.ds(0, 12)])
    cot_all = cf[...].reshape(512, 512)
    for h in range(4):
        back[h] = dot(weight(h, 1), cot_all)

    arrived(G2, gf.at[pl.ds(0, 12)])
    gate_all = gf[...].reshape(512, 512)
    for h in range(4):
        value, slope = gelu_parts(dot(weight(h, 0), gate_all))
        hid[h] = value.astype(BF16)
        pg[h] = (back[h] * slope).astype(BF16)

    def partials(weights, units, dst):
        all_units = units[...].reshape(512, 512)
        for b in range(4):
            dst[b] = dot(weights[b], all_units).reshape(4, 32, 512).astype(BF16)

    def total(parts):
        value = parts[0].astype(F32)
        for part in parts[1:]:
            value = value + part.astype(F32)
        return value

    partials(w1t, pg, su)
    for o in (2, 1, 3, 0):
        to, _ = along_z(o)
        for d in (1, 2, 3):
            x = lax.rem(cx + d, 4)
            send(U1 + o, su.at[x, to], ru.at[o, cx], s, 4 * x + cz)
        ru[o, cx] = su[cx, to]
        pending.append((U1 + o, ru.at[0, pl.ds(0, 3)]))

    for h in range(4):
        for n, (units, fed) in enumerate(((pg, gate_all), (hid, cot_all))):
            rows = dot(units[h], fed, NT).astype(BF16)
            sg[0, h, n] = rows[0:64]
            sg[1, h, n] = rows[64:128]
    send(PC, sg.at[1 - core], sx, other, c)
    pending.append((PC, sx))

    for o in (2, 1, 3, 0):
        to, _ = along_z(o)
        arrived(U1 + o, ru.at[0, pl.ds(0, 3)])
        value = total([ru[o, x] for x in range(4)]).astype(BF16)
        if o == 0:
            ru2[cz] = value
        else:
            su2[o] = value
            send(U2, su2.at[o], ru2.at[cz], s, 4 * cx + to)
    pending.append((U2, ru2.at[pl.ds(0, 3)]))

    arrived(PC, sx)
    sp[...] = (sg[core].astype(F32) + sx[...].astype(F32)).astype(BF16)
    rp[cz] = sp[cz]
    for o in (2, 1, 3):
        to, _ = along_z(o)
        send(PZ, sp.at[to], rp.at[cz], s, 4 * cx + to)
    pending.append((PZ, rp.at[pl.ds(0, 3)]))

    partials(w2t, hid, sm)
    for d in (1, 2, 3):
        x = lax.rem(cx + d, 4)
        send(M1, sm.at[x], rm.at[cx], s, 4 * x + cz)
    rm[cx] = sm[cx]
    pending.append((M1, rm.at[pl.ds(0, 3)]))

    arrived(U2, ru2.at[pl.ds(0, 3)])
    rows = []
    for l in range(8):
        at = slice(256 * (l % 2), 256 * (l % 2) + 256)
        t = tokp[l].astype(F32)
        g = cots[l // 2, :, at].astype(F32) + ru2[l // 2, :, at].astype(F32)
        gg[l] = g
        rows.append(g * (t * jax.nn.sigmoid(t)))
    flip(rows, s3)
    r3[s] = s3[s]
    over_seq(A3, lambda t: s3.at[t], r3)

    arrived(M1, rm.at[pl.ds(0, 3)])
    sm2[...] = total([rm[x] for x in range(4)]).astype(BF16)
    rm2[cz] = sm2[cz]
    for o in (2, 1, 3):
        to, _ = along_z(o)
        send(M2, sm2.at[to], rm2.at[cz], s, 4 * cx + to)
    pending.append((M2, rm2.at[pl.ds(0, 3)]))

    arrived(PZ, rp.at[pl.ds(0, 3)])
    sh[...] = total([rp[z] for z in range(4)]).reshape(16, 8, 512).astype(BF16)
    rh[pair] = sh[pair]

    @pl.loop(1, 16)
    def _(o):
        t = lax.rem(pair + o, 16)
        send(PS, sh.at[t], rh.at[pair], 2 * t + core, c)

    pending.append((PS, rh.at[pl.ds(0, 15)]))

    arrived(A3, r3.at[pl.ds(0, NS - 1)])
    fold_src[...] = r3[...].astype(F32)
    flip([dot(dot(fold_t, spread(k), NT).astype(BF16), l_v[k]) for k in range(8)], s4)
    r4[s] = s4[s]
    over_seq(A4, lambda t: s4.at[t], r4)

    arrived(PS, rh.at[pl.ds(0, 15)])
    sf[...] = jnp.sum(rh[...].astype(F32), axis=0).astype(BF16)
    rf[s] = sf[...]
    over_seq(PA, lambda t: sf, rf)

    for k in range(8):
        g = dot(spread(k), fold_t, NT).astype(BF16)
        gl_v[k] = dot(g, ct[k]).astype(BF16)

    arrived(M2, rm2.at[pl.ds(0, 3)])
    for l in range(8):
        at = slice(256 * (l % 2), 256 * (l % 2) + 256)
        value = (go[l // 2, :, at].astype(F32) + rm2[l // 2, :, at].astype(F32)).astype(BF16)
        mixed_v[:, 256 * l : 256 * l + 256] = value[0:GC]
    outs = [pltpu.make_async_copy(gl_v, gl_h, out_sem.at[0]), pltpu.make_async_copy(mixed_v, mixed_h, out_sem.at[1])]
    for copy in outs:
        copy.start()

    arrived(A4, r4.at[pl.ds(0, NS - 1)])
    fold_src[...] = r4[...].astype(F32)
    for i in range(8):
        x = spread(i)
        g = dot(x, fold_t, NT).astype(BF16)
        g_t = dot(fold_t, x, NT).astype(BF16)
        gr_v[i] = dot(g, tokp[i]).astype(BF16)
        t = tokp[i].astype(F32)
        sigma = jax.nn.sigmoid(t)
        through = gg[i] * (1.0 + mon[i] * (sigma * (1.0 + t * (1.0 - sigma))))
        value = (through + dot(g_t, r_v[i])).astype(BF16)
        gin_v[:, 256 * i : 256 * i + 256] = value[0:GC]
    outs += [pltpu.make_async_copy(gr_v, gr_h, out_sem.at[2]), pltpu.make_async_copy(gin_v, gin_h, out_sem.at[3])]
    for copy in outs[2:]:
        copy.start()

    arrived(PA, rf.at[pl.ds(0, NS - 1)])
    halves = rf[...].reshape(16, 2, 8, 512)
    g_in = jnp.concatenate([halves[0:8, k].reshape(64, 512) for k in range(2)], axis=0)
    g_out = jnp.concatenate([halves[8:16, k].reshape(64, 512) for k in range(2)], axis=0)
    gwi_v[...] = dot(pad_cols, g_in, NT)[:, 0:HID].astype(BF16)
    gwo_v[...] = dot(g_out, pad_cols, NT)[0:HID].astype(BF16)
    outs += [pltpu.make_async_copy(gwi_v, gwi_h, out_sem.at[4]), pltpu.make_async_copy(gwo_v, gwo_h, out_sem.at[5])]
    for copy in outs[4:]:
        copy.start()

    for which, view in pending:
        sent(which, view)
    for copy in outs:
        copy.wait()


def hand_over(*refs):
    held, into, out = refs[12:18], refs[18], refs[19]
    reads = [pltpu.make_async_copy(refs[m], held[m], into.at[m]) for m in range(6)]
    writes = [pltpu.make_async_copy(held[m], refs[6 + m], out.at[m]) for m in range(6)]
    for copy in reads:
        copy.start()
    for read, write in zip(reads, writes):
        read.wait()
        write.start()
    for copy in writes:
        copy.wait()


def local(tokens, cotangent, right_blocks, left_blocks, w_in, w_out):
    piece = (NS, 8, 256)
    scratch = [
        ((GC, 2048), BF16), ((GC, 2048), BF16), ((8, 256, 256), BF16), ((8, 256, 256), BF16),
        ((480, HID), BF16), ((HID, 480), BF16),
        ((8, 32, 256), BF16), ((4, 32, 512), BF16),
        (piece, BF16), (piece, BF16), (piece, BF16), (piece, BF16),
        (piece, BF16), (piece, BF16), (piece, BF16), (piece, BF16),
        (piece, F32), ((8, 32, 256), BF16), ((8, 32, 256), F32),
        ((4, 32, 512), BF16), ((16, 32, 512), BF16), ((16, 32, 512), BF16),
        ((2, 2, 64, 512), BF16), ((2, 4, 2, 64, 512), BF16),
        ((4, 128, 512), BF16), ((4, 128, 512), BF16), ((4, 128, 512), F32),
        ((4, 128, 512), BF16), ((4, 128, 512), BF16),
        ((4, 4, 32, 512), BF16), ((4, 4, 32, 512), BF16), ((4, 32, 512), BF16), ((4, 32, 512), BF16),
        ((4, 4, 32, 512), BF16), ((4, 4, 32, 512), BF16), ((4, 32, 512), BF16), ((4, 32, 512), BF16),
        ((2, 4, 2, 64, 512), BF16), ((4, 2, 64, 512), BF16), ((4, 2, 64, 512), BF16), ((4, 2, 64, 512), BF16),
        ((16, 8, 512), BF16), ((16, 8, 512), BF16), ((8, 512), BF16), ((NS, 8, 512), BF16),
        ((8, 32, 256), F32),
        ((GC, 2048), BF16), ((GC, 2048), BF16), ((8, 256, 256), BF16), ((8, 256, 256), BF16),
        ((480, HID), BF16), ((HID, 480), BF16),
    ]
    shapes = [
        ((GC, 2048), BF16), ((GC, 2048), BF16), ((8, 256, 256), BF16), ((8, 256, 256), BF16),
        ((480, HID), BF16), ((HID, 480), BF16),
    ]
    results = pl.pallas_call(
        kernel,
        out_shape=[jax.ShapeDtypeStruct(*shape) for shape in shapes],
        in_specs=[pl.BlockSpec(memory_space=pl.ANY)] * 6,
        out_specs=[pl.BlockSpec(memory_space=pl.ANY)] * 6,
        scratch_shapes=[pltpu.VMEM(*shape) for shape in scratch]
        + [pltpu.SemaphoreType.DMA((6,)), pltpu.SemaphoreType.DMA((6,))]
        + [pltpu.SemaphoreType.DMA((N_SEM,)), pltpu.SemaphoreType.DMA((N_SEM,))],
        compiler_params=pltpu.CompilerParams(
            collective_id=0, has_side_effects=True, vmem_limit_bytes=VMEM_LIMIT
        ),
        name="monarch_block",
    )(tokens, cotangent, right_blocks[0], left_blocks[0], w_in, w_out)
    mixed, gin, gr, gl, gwi, gwo = pl.pallas_call(
        hand_over,
        out_shape=[jax.ShapeDtypeStruct(*shape) for shape in shapes],
        in_specs=[pl.BlockSpec(memory_space=pl.ANY)] * 6,
        out_specs=[pl.BlockSpec(memory_space=pl.ANY)] * 6,
        scratch_shapes=[pltpu.VMEM(*shape) for shape in shapes] + [pltpu.SemaphoreType.DMA((6,))] * 2,
        compiler_params=pltpu.CompilerParams(vmem_limit_bytes=VMEM_LIMIT),
        name="hand_over",
    )(*results)
    return mixed, gin, gr[None], gl[None], gwi, gwo


def solution(mesh):
    placed = (
        P("ch", "seq"),
        P("ch", "seq"),
        P("ch", "seq", None, None),
        P("ch", "seq", None, None),
        P(None, "ch"),
        P("ch", None),
    )
    return jax.shard_map(
        local,
        mesh=mesh,
        in_specs=placed,
        out_specs=placed,
        check_vma=False,
    )
```

```python
import jax
import jax.numpy as jnp
from jax import lax
from jax.experimental import pallas as pl
from jax.experimental.pallas import tpu as pltpu
from jax.sharding import PartitionSpec as P

NS = 32
NC = 16
GC = 30
HID = 120
VMEM_LIMIT = 60 * 1024 * 1024
F32 = jnp.float32
BF16 = jnp.bfloat16
MESH = pl.DeviceIdType.MESH

NN = (((1,), (0,)), ((), ()))
NT = (((1,), (1,)), ((), ()))
TN = (((0,), (0,)), ((), ()))

A1, A2, A3, A4 = 0, 1, 2, 3
C1, C2, G1, G2 = 4, 8, 9, 13
WZ, WC = 14, 15
U1, U2, M1, M2 = 16, 20, 21, 22
PC, PS, PZ, PA = 23, 27, 28, 29
N_SEM = 30


def dot(a, b, dims=NN):
    return lax.dot_general(a, b, dims, preferred_element_type=F32)


def one_hot(shape, test):
    rows = lax.broadcasted_iota(jnp.int32, shape, 0)
    cols = lax.broadcasted_iota(jnp.int32, shape, 1)
    return jnp.where(test(rows, cols), 1.0, 0.0).astype(BF16)


def gelu_parts(v):
    cdf = 0.5 * (1.0 + lax.erf(v * 0.7071067811865476))
    return v * cdf, cdf + v * jnp.exp(-0.5 * v * v) * 0.3989422804014327


def kernel(
    tok_h, cot_h, r_h, l_h, wi_h, wo_h,
    mixed_h, gin_h, gr_h, gl_h, gwi_h, gwo_h,
    tok_v, cot_v, r_v, l_v, wi_v, wo_v,
    tokp, cots, s1, r1, s2, r2, s3, r3, s4, r4,
    fold_src, ct, mon, go, gf, cf, ws, w12, w1t, w2t, back, hid, pg,
    su, ru, su2, ru2, sm, rm, sm2, rm2,
    sg, sx, sp, rp, sq, rq, sf, rf, gg,
    mixed_v, gin_v, gl_v, gr_v, gwi_v, gwo_v,
    in_sem, out_sem, send_sem, recv_sem,
):
    s, c = lax.axis_index("seq"), lax.axis_index("ch")
    cx, cz = c // 4, lax.rem(c, 4)
    core = lax.rem(s, 2)
    pair = s // 2
    other = s + 1 - 2 * core

    barrier = pltpu.get_barrier_semaphore()

    @pl.loop(1, NS)
    def _(o):
        pl.semaphore_signal(barrier, inc=1, device_id={"seq": lax.rem(s + o, NS), "ch": c}, device_id_type=MESH)

    @pl.loop(1, NC)
    def _(o):
        pl.semaphore_signal(barrier, inc=1, device_id={"seq": s, "ch": lax.rem(c + o, NC)}, device_id_type=MESH)

    ins = [
        pltpu.make_async_copy(src, dst, in_sem.at[n])
        for n, (src, dst) in enumerate(
            ((tok_h, tok_v), (r_h, r_v), (cot_h, cot_v), (wi_h, wi_v), (wo_h, wo_v), (l_h, l_v))
        )
    ]
    for copy in ins:
        copy.start()

    pending = []

    def send(which, src, dst, seq, ch):
        pltpu.make_async_remote_copy(
            src_ref=src, dst_ref=dst, send_sem=send_sem.at[which], recv_sem=recv_sem.at[which],
            device_id={"seq": seq, "ch": ch}, device_id_type=MESH,
        ).start()

    def over_seq(which, src_of, dst):
        @pl.loop(1, NS)
        def _(o):
            t = lax.rem(s + o, NS)
            send(which, src_of(t), dst.at[s], t, c)

        pending.append((which, dst.at[pl.ds(0, NS - 1)]))

    def along_x(which, src, dst):
        for o in (1, 2, 3):
            send(which, src, dst, s, lax.rem(cx + o, 4) * 4 + cz)

    def along_z(o):
        return lax.rem(cz + o, 4), lax.rem(cz + 4 - o, 4)

    def arrived(which, view):
        pltpu.make_async_copy(view, view, recv_sem.at[which]).wait()

    def sent(which, view):
        pltpu.make_async_copy(view, view, send_sem.at[which]).wait()

    def gather_first(z_sem, x_sem, src, dst):
        for o in (2, 1, 3):
            to, _ = along_z(o)
            send(z_sem + o, src.at[to], dst.at[c], s, 4 * cx + to)
            pending.append((z_sem + o, dst.at[0]))
        dst[c] = src[cz]
        along_x(x_sem, src.at[cz], dst.at[c])

    def gather_second(z_sem, x_sem, dst):
        for o in (1, 3, 2):
            _, frm = along_z(o)
            arrived(z_sem + o, dst.at[0])
            along_x(x_sem, dst.at[4 * cx + frm], dst.at[4 * cx + frm])
        pending.append((x_sem, dst.at[pl.ds(0, 12)]))

    eye = one_hot((256, 256), lambda a, b: a == b)
    fold_t = one_hot((32, 256), lambda a, b: a == (b & 31))
    keep = (
        (lax.broadcasted_iota(jnp.int32, (8, 256), 1) >> 5) == lax.broadcasted_iota(jnp.int32, (8, 256), 0)
    )[None]

    def spread(n):
        row = jnp.broadcast_to(fold_src[:, n : n + 1, :], (NS, 8, 256))
        return jnp.where(keep, row, 0.0).reshape(256, 256).astype(BF16)

    def flip(rows, dst):
        stacked = jnp.concatenate([row.astype(BF16) for row in rows], axis=0)
        dst[...] = dot(eye, stacked, NT).reshape(NS, 8, 256).astype(BF16)

    ins[0].wait()
    tokp[...] = jnp.zeros_like(tokp)
    for i in range(8):
        tokp[i, 0:GC, :] = tok_v[:, 256 * i : 256 * i + 256]
    ins[1].wait()
    flip([dot(tokp[i], r_v[i], NT) for i in range(8)], s1)
    r1[s] = s1[s]
    pl.semaphore_wait(barrier, NS + NC - 2)
    over_seq(A1, lambda t: s1.at[t], r1)

    ins[2].wait()
    cots[...] = jnp.zeros_like(cots)
    for q in range(4):
        cots[q, 0:GC, :] = cot_v[:, 512 * q : 512 * q + 512]
    gather_first(C1, C2, cots, cf)
    pad_cols = one_hot(
        (GC * NC, 512), lambda a, b: (a == GC * (b >> 5) + (b & 31)) & ((b & 31) < GC)
    )
    ins[3].wait()
    ins[4].wait()
    for n, rows in enumerate((dot(wi_v[...], pad_cols, TN), dot(wo_v[...], pad_cols))):
        ws[0, n] = rows[0:64].astype(BF16)
        ws[1, n] = jnp.zeros((64, 512), BF16)
        ws[1, n, 0 : HID - 64, :] = rows[64:HID].astype(BF16)
    w12[core, cz] = ws[core]
    for o in (1, 2, 3):
        to, _ = along_z(o)
        send(WZ, ws.at[core], w12.at[core, cz], s, 4 * cx + to)
    pending.append((WZ, w12.at[0, pl.ds(0, 3)]))

    ins[5].wait()
    arrived(A1, r1.at[pl.ds(0, NS - 1)])
    fold_src[...] = r1[...].astype(F32)
    for k in range(8):
        ct[k] = dot(fold_t, spread(k), NT).astype(BF16)
    flip([dot(ct[k], l_v[k], NT) for k in range(8)], s2)
    r2[s] = s2[s]
    over_seq(A2, lambda t: s2.at[t], r2)
    gather_second(C1, C2, cf)

    arrived(A2, r2.at[pl.ds(0, NS - 1)])
    fold_src[...] = r2[...].astype(F32)
    for l in range(8):
        m = dot(fold_t, spread(l), NT)
        mon[l] = m
        t = tokp[l].astype(F32)
        go[l // 2, :, 256 * (l % 2) : 256 * (l % 2) + 256] = (t + m * (t * jax.nn.sigmoid(t))).astype(BF16)
    gather_first(G1, G2, go, gf)
    arrived(WZ, w12.at[0, pl.ds(0, 3)])
    send(WC, w12.at[core], w12.at[core], other, c)
    pending.append((WC, w12.at[0]))
    gather_second(G1, G2, gf)

    arrived(WC, w12.at[0])
    eye128 = one_hot((128, 128), lambda a, b: a == b)

    def weight(h, n):
        return w12[:, h, n].reshape(128, 512)

    for h in range(4):
        for n, turned in enumerate((w1t, w2t)):
            held = weight(h, n)
            for b in range(4):
                turned[b, :, 128 * h : 128 * h + 128] = dot(
                    eye128, held[:, 128 * b : 128 * b + 128], NT
                ).astype(BF16)
    arrived(C2, cf.at[pl.ds(0, 12)])
    cot_all = cf[...].reshape(512, 512)
    for h in range(4):
        back[h] = dot(weight(h, 1), cot_all)

    arrived(G2, gf.at[pl.ds(0, 12)])
    gate_all = gf[...].reshape(512, 512)
    for h in range(4):
        value, slope = gelu_parts(dot(weight(h, 0), gate_all))
        hid[h] = value.astype(BF16)
        pg[h] = (back[h] * slope).astype(BF16)

    def partials(weights, units, dst):
        all_units = units[...].reshape(512, 512)
        for b in range(4):
            dst[b] = dot(weights[b], all_units).reshape(4, 32, 512).astype(BF16)

    def total(parts):
        value = parts[0].astype(F32)
        for part in parts[1:]:
            value = value + part.astype(F32)
        return value

    partials(w1t, pg, su)
    for o in (2, 1, 3, 0):
        to, _ = along_z(o)
        for d in (1, 2, 3):
            x = lax.rem(cx + d, 4)
            send(U1 + o, su.at[x, to], ru.at[o, cx], s, 4 * x + cz)
        ru[o, cx] = su[cx, to]
        pending.append((U1 + o, ru.at[0, pl.ds(0, 3)]))

    for o in (2, 1, 3, 0):
        to, _ = along_z(o)
        for n, (units, fed) in enumerate(((pg, gate_all), (hid, cot_all))):
            rows = dot(units[to], fed, NT).reshape(16, 8, 512).astype(BF16)
            sg[0, to, 8 * n : 8 * n + 8] = rows[0:8]
            sg[1, to, 8 * n : 8 * n + 8] = rows[8:16]
        send(PC + o, sg.at[1 - core, to], sx.at[to], other, c)
        pending.append((PC + o, sx.at[0]))

    for o in (2, 1, 3, 0):
        to, _ = along_z(o)
        arrived(PC + o, sx.at[0])
        sp[to] = (sg[core, to].astype(F32) + sx[to].astype(F32)).astype(BF16)

        @pl.loop(1, 16)
        def _(n):
            t = lax.rem(pair + n, 16)
            send(PS, sp.at[to, t], rp.at[pair, to], 2 * t + core, c)

    for z in range(4):
        rp[pair, z] = sp[z, pair]
    pending.append((PS, rp.at[pl.ds(0, 15)]))

    for o in (2, 1, 3, 0):
        to, _ = along_z(o)
        arrived(U1 + o, ru.at[0, pl.ds(0, 3)])
        value = total([ru[o, x] for x in range(4)]).astype(BF16)
        if o == 0:
            ru2[cz] = value
        else:
            su2[o] = value
            send(U2, su2.at[o], ru2.at[cz], s, 4 * cx + to)
    pending.append((U2, ru2.at[pl.ds(0, 3)]))

    partials(w2t, hid, sm)
    for d in (1, 2, 3):
        x = lax.rem(cx + d, 4)
        send(M1, sm.at[x], rm.at[cx], s, 4 * x + cz)
    rm[cx] = sm[cx]
    pending.append((M1, rm.at[pl.ds(0, 3)]))

    arrived(U2, ru2.at[pl.ds(0, 3)])
    rows = []
    for l in range(8):
        at = slice(256 * (l % 2), 256 * (l % 2) + 256)
        t = tokp[l].astype(F32)
        g = cots[l // 2, :, at].astype(F32) + ru2[l // 2, :, at].astype(F32)
        gg[l] = g
        rows.append(g * (t * jax.nn.sigmoid(t)))
    flip(rows, s3)
    r3[s] = s3[s]
    over_seq(A3, lambda t: s3.at[t], r3)

    arrived(M1, rm.at[pl.ds(0, 3)])
    sm2[...] = total([rm[x] for x in range(4)]).astype(BF16)
    rm2[cz] = sm2[cz]
    for o in (2, 1, 3):
        to, _ = along_z(o)
        send(M2, sm2.at[to], rm2.at[cz], s, 4 * cx + to)
    pending.append((M2, rm2.at[pl.ds(0, 3)]))

    arrived(PS, rp.at[pl.ds(0, 15)])
    sq[...] = jnp.sum(rp[...].astype(F32), axis=0).astype(BF16)
    rq[cz] = sq[cz]
    for o in (2, 1, 3):
        to, _ = along_z(o)
        send(PZ, sq.at[to], rq.at[cz], s, 4 * cx + to)
    pending.append((PZ, rq.at[pl.ds(0, 3)]))

    arrived(A3, r3.at[pl.ds(0, NS - 1)])
    fold_src[...] = r3[...].astype(F32)
    flip([dot(dot(fold_t, spread(k), NT).astype(BF16), l_v[k]) for k in range(8)], s4)
    r4[s] = s4[s]
    over_seq(A4, lambda t: s4.at[t], r4)

    arrived(PZ, rq.at[pl.ds(0, 3)])
    sf[...] = total([rq[z] for z in range(4)]).astype(BF16)
    rf[s] = sf[...]
    over_seq(PA, lambda t: sf, rf)

    for k in range(8):
        g = dot(spread(k), fold_t, NT).astype(BF16)
        gl_v[k] = dot(g, ct[k]).astype(BF16)

    arrived(M2, rm2.at[pl.ds(0, 3)])
    for l in range(8):
        at = slice(256 * (l % 2), 256 * (l % 2) + 256)
        value = (go[l // 2, :, at].astype(F32) + rm2[l // 2, :, at].astype(F32)).astype(BF16)
        mixed_v[:, 256 * l : 256 * l + 256] = value[0:GC]
    outs = [pltpu.make_async_copy(gl_v, gl_h, out_sem.at[0]), pltpu.make_async_copy(mixed_v, mixed_h, out_sem.at[1])]
    for copy in outs:
        copy.start()

    arrived(A4, r4.at[pl.ds(0, NS - 1)])
    fold_src[...] = r4[...].astype(F32)
    for i in range(8):
        x = spread(i)
        g = dot(x, fold_t, NT).astype(BF16)
        g_t = dot(fold_t, x, NT).astype(BF16)
        gr_v[i] = dot(g, tokp[i]).astype(BF16)
        t = tokp[i].astype(F32)
        sigma = jax.nn.sigmoid(t)
        through = gg[i] * (1.0 + mon[i] * (sigma * (1.0 + t * (1.0 - sigma))))
        value = (through + dot(g_t, r_v[i])).astype(BF16)
        gin_v[:, 256 * i : 256 * i + 256] = value[0:GC]
    outs += [pltpu.make_async_copy(gr_v, gr_h, out_sem.at[2]), pltpu.make_async_copy(gin_v, gin_h, out_sem.at[3])]
    for copy in outs[2:]:
        copy.start()

    arrived(PA, rf.at[pl.ds(0, NS - 1)])
    halves = rf[...].reshape(16, 2, 8, 512)
    g_in = jnp.concatenate([halves[0:8, k].reshape(64, 512) for k in range(2)], axis=0)
    g_out = jnp.concatenate([halves[8:16, k].reshape(64, 512) for k in range(2)], axis=0)
    gwi_v[...] = dot(pad_cols, g_in, NT)[:, 0:HID].astype(BF16)
    gwo_v[...] = dot(g_out, pad_cols, NT)[0:HID].astype(BF16)
    outs += [pltpu.make_async_copy(gwi_v, gwi_h, out_sem.at[4]), pltpu.make_async_copy(gwo_v, gwo_h, out_sem.at[5])]
    for copy in outs[4:]:
        copy.start()

    for which, view in pending:
        sent(which, view)
    for copy in outs:
        copy.wait()


def hand_over(*refs):
    held, into, out = refs[12:18], refs[18], refs[19]
    reads = [pltpu.make_async_copy(refs[m], held[m], into.at[m]) for m in range(6)]
    writes = [pltpu.make_async_copy(held[m], refs[6 + m], out.at[m]) for m in range(6)]
    for copy in reads:
        copy.start()
    for read, write in zip(reads, writes):
        read.wait()
        write.start()
    for copy in writes:
        copy.wait()


def local(tokens, cotangent, right_blocks, left_blocks, w_in, w_out):
    piece = (NS, 8, 256)
    scratch = [
        ((GC, 2048), BF16), ((GC, 2048), BF16), ((8, 256, 256), BF16), ((8, 256, 256), BF16),
        ((480, HID), BF16), ((HID, 480), BF16),
        ((8, 32, 256), BF16), ((4, 32, 512), BF16),
        (piece, BF16), (piece, BF16), (piece, BF16), (piece, BF16),
        (piece, BF16), (piece, BF16), (piece, BF16), (piece, BF16),
        (piece, F32), ((8, 32, 256), BF16), ((8, 32, 256), F32),
        ((4, 32, 512), BF16), ((16, 32, 512), BF16), ((16, 32, 512), BF16),
        ((2, 2, 64, 512), BF16), ((2, 4, 2, 64, 512), BF16),
        ((4, 128, 512), BF16), ((4, 128, 512), BF16), ((4, 128, 512), F32),
        ((4, 128, 512), BF16), ((4, 128, 512), BF16),
        ((4, 4, 32, 512), BF16), ((4, 4, 32, 512), BF16), ((4, 32, 512), BF16), ((4, 32, 512), BF16),
        ((4, 4, 32, 512), BF16), ((4, 4, 32, 512), BF16), ((4, 32, 512), BF16), ((4, 32, 512), BF16),
        ((2, 4, 16, 8, 512), BF16), ((4, 16, 8, 512), BF16), ((4, 16, 8, 512), BF16), ((16, 4, 8, 512), BF16),
        ((4, 8, 512), BF16), ((4, 8, 512), BF16), ((8, 512), BF16), ((NS, 8, 512), BF16),
        ((8, 32, 256), F32),
        ((GC, 2048), BF16), ((GC, 2048), BF16), ((8, 256, 256), BF16), ((8, 256, 256), BF16),
        ((480, HID), BF16), ((HID, 480), BF16),
    ]
    shapes = [
        ((GC, 2048), BF16), ((GC, 2048), BF16), ((8, 256, 256), BF16), ((8, 256, 256), BF16),
        ((480, HID), BF16), ((HID, 480), BF16),
    ]
    results = pl.pallas_call(
        kernel,
        out_shape=[jax.ShapeDtypeStruct(*shape) for shape in shapes],
        in_specs=[pl.BlockSpec(memory_space=pl.ANY)] * 6,
        out_specs=[pl.BlockSpec(memory_space=pl.ANY)] * 6,
        scratch_shapes=[pltpu.VMEM(*shape) for shape in scratch]
        + [pltpu.SemaphoreType.DMA((6,)), pltpu.SemaphoreType.DMA((6,))]
        + [pltpu.SemaphoreType.DMA((N_SEM,)), pltpu.SemaphoreType.DMA((N_SEM,))],
        compiler_params=pltpu.CompilerParams(
            collective_id=0, has_side_effects=True, vmem_limit_bytes=VMEM_LIMIT
        ),
        name="monarch_block",
    )(tokens, cotangent, right_blocks[0], left_blocks[0], w_in, w_out)
    mixed, gin, gr, gl, gwi, gwo = pl.pallas_call(
        hand_over,
        out_shape=[jax.ShapeDtypeStruct(*shape) for shape in shapes],
        in_specs=[pl.BlockSpec(memory_space=pl.ANY)] * 6,
        out_specs=[pl.BlockSpec(memory_space=pl.ANY)] * 6,
        scratch_shapes=[pltpu.VMEM(*shape) for shape in shapes] + [pltpu.SemaphoreType.DMA((6,))] * 2,
        compiler_params=pltpu.CompilerParams(vmem_limit_bytes=VMEM_LIMIT),
        name="hand_over",
    )(*results)
    return mixed, gin, gr[None], gl[None], gwi, gwo


def solution(mesh):
    placed = (
        P("ch", "seq"),
        P("ch", "seq"),
        P("ch", "seq", None, None),
        P("ch", "seq", None, None),
        P(None, "ch"),
        P("ch", None),
    )
    return jax.shard_map(
        local,
        mesh=mesh,
        in_specs=placed,
        out_specs=placed,
        check_vma=False,
    )
```

```python
import jax
import jax.numpy as jnp
from jax import lax
from jax.experimental import pallas as pl
from jax.experimental.pallas import tpu as pltpu
from jax.sharding import PartitionSpec as P

NS = 32
NC = 16
GC = 30
HID = 120
VMEM_LIMIT = 60 * 1024 * 1024
F32 = jnp.float32
BF16 = jnp.bfloat16
MESH = pl.DeviceIdType.MESH

NN = (((1,), (0,)), ((), ()))
NT = (((1,), (1,)), ((), ()))
TN = (((0,), (0,)), ((), ()))

A1, A2, A3, A4 = 0, 1, 2, 3
C1, C2, G1, G2 = 4, 8, 9, 13
WZ, WC = 14, 15
U1, U2, M1, M2 = 16, 20, 21, 22
PC, PS, PZ, PA = 23, 27, 28, 29
N_SEM = 30


def dot(a, b, dims=NN):
    return lax.dot_general(a, b, dims, preferred_element_type=F32)


def one_hot(shape, test):
    rows = lax.broadcasted_iota(jnp.int32, shape, 0)
    cols = lax.broadcasted_iota(jnp.int32, shape, 1)
    return jnp.where(test(rows, cols), 1.0, 0.0).astype(BF16)


def gelu_parts(v):
    cdf = 0.5 * (1.0 + lax.erf(v * 0.7071067811865476))
    return v * cdf, cdf + v * jnp.exp(-0.5 * v * v) * 0.3989422804014327


def kernel(
    tok_h, cot_h, r_h, l_h, wi_h, wo_h,
    mixed_h, gin_h, gr_h, gl_h, gwi_h, gwo_h,
    tok_v, cot_v, r_v, l_v, wi_v, wo_v,
    tokp, cots, s1, r1, s2, r2, s3, r3, s4, r4,
    fold_src, ct, mon, go, gf, cf, ws, w12, w1t, w2t, back, hid, pg,
    su, ru, su2, ru2, sm, rm, sm2, rm2,
    sg, sx, sp, rp, sq, rq, sf, rf, gg,
    mixed_v, gin_v, gl_v, gr_v, gwi_v, gwo_v,
    in_sem, out_sem, send_sem, recv_sem,
):
    s, c = lax.axis_index("seq"), lax.axis_index("ch")
    cx, cz = c // 4, lax.rem(c, 4)
    core = lax.rem(s, 2)
    pair = s // 2
    other = s + 1 - 2 * core

    barrier = pltpu.get_barrier_semaphore()

    @pl.loop(1, NS)
    def _(o):
        pl.semaphore_signal(barrier, inc=1, device_id={"seq": lax.rem(s + o, NS), "ch": c}, device_id_type=MESH)

    @pl.loop(1, NC)
    def _(o):
        pl.semaphore_signal(barrier, inc=1, device_id={"seq": s, "ch": lax.rem(c + o, NC)}, device_id_type=MESH)

    ins = [
        pltpu.make_async_copy(src, dst, in_sem.at[n])
        for n, (src, dst) in enumerate(
            ((tok_h, tok_v), (r_h, r_v), (cot_h, cot_v), (wi_h, wi_v), (wo_h, wo_v), (l_h, l_v))
        )
    ]
    for copy in ins:
        copy.start()

    pending = []

    def send(which, src, dst, seq, ch):
        pltpu.make_async_remote_copy(
            src_ref=src, dst_ref=dst, send_sem=send_sem.at[which], recv_sem=recv_sem.at[which],
            device_id={"seq": seq, "ch": ch}, device_id_type=MESH,
        ).start()

    def over_seq(which, src_of, dst):
        @pl.loop(1, NS)
        def _(o):
            t = lax.rem(s + o, NS)
            send(which, src_of(t), dst.at[s], t, c)

        pending.append((which, dst.at[pl.ds(0, NS - 1)]))

    def along_x(which, src, dst):
        for o in (1, 2, 3):
            send(which, src, dst, s, lax.rem(cx + o, 4) * 4 + cz)

    def along_z(o):
        return lax.rem(cz + o, 4), lax.rem(cz + 4 - o, 4)

    def arrived(which, view):
        pltpu.make_async_copy(view, view, recv_sem.at[which]).wait()

    def sent(which, view):
        pltpu.make_async_copy(view, view, send_sem.at[which]).wait()

    def gather_first(z_sem, x_sem, src, dst):
        for o in (2, 1, 3):
            to, _ = along_z(o)
            send(z_sem + o, src.at[to], dst.at[c], s, 4 * cx + to)
            pending.append((z_sem + o, dst.at[0]))
        dst[c] = src[cz]
        along_x(x_sem, src.at[cz], dst.at[c])

    def gather_second(z_sem, x_sem, dst):
        for o in (1, 3, 2):
            _, frm = along_z(o)
            arrived(z_sem + o, dst.at[0])
            along_x(x_sem, dst.at[4 * cx + frm], dst.at[4 * cx + frm])
        pending.append((x_sem, dst.at[pl.ds(0, 12)]))

    eye = one_hot((256, 256), lambda a, b: a == b)
    fold_t = one_hot((32, 256), lambda a, b: a == (b & 31))
    keep = (
        (lax.broadcasted_iota(jnp.int32, (8, 256), 1) >> 5) == lax.broadcasted_iota(jnp.int32, (8, 256), 0)
    )[None]

    def spread(n):
        row = jnp.broadcast_to(fold_src[:, n : n + 1, :], (NS, 8, 256))
        return jnp.where(keep, row, 0.0).reshape(256, 256).astype(BF16)

    def flip(rows, dst):
        stacked = jnp.concatenate([row.astype(BF16) for row in rows], axis=0)
        dst[...] = dot(eye, stacked, NT).reshape(NS, 8, 256).astype(BF16)

    ins[0].wait()
    tokp[...] = jnp.zeros_like(tokp)
    for i in range(8):
        tokp[i, 0:GC, :] = tok_v[:, 256 * i : 256 * i + 256]
    ins[1].wait()
    flip([dot(tokp[i], r_v[i], NT) for i in range(8)], s1)
    r1[s] = s1[s]
    pl.semaphore_wait(barrier, NS + NC - 2)
    over_seq(A1, lambda t: s1.at[t], r1)

    ins[2].wait()
    cots[...] = jnp.zeros_like(cots)
    for q in range(4):
        cots[q, 0:GC, :] = cot_v[:, 512 * q : 512 * q + 512]
    gather_first(C1, C2, cots, cf)
    pad_cols = one_hot(
        (GC * NC, 512), lambda a, b: (a == GC * (b >> 5) + (b & 31)) & ((b & 31) < GC)
    )
    ins[3].wait()
    ins[4].wait()
    for n, rows in enumerate((dot(wi_v[...], pad_cols, TN), dot(wo_v[...], pad_cols))):
        ws[0, n] = rows[0:64].astype(BF16)
        ws[1, n] = jnp.zeros((64, 512), BF16)
        ws[1, n, 0 : HID - 64, :] = rows[64:HID].astype(BF16)
    w12[core, cz] = ws[core]
    for o in (1, 2, 3):
        to, _ = along_z(o)
        send(WZ, ws.at[core], w12.at[core, cz], s, 4 * cx + to)
    pending.append((WZ, w12.at[0, pl.ds(0, 3)]))

    ins[5].wait()
    arrived(A1, r1.at[pl.ds(0, NS - 1)])
    fold_src[...] = r1[...].astype(F32)
    for k in range(8):
        ct[k] = dot(fold_t, spread(k), NT).astype(BF16)
    flip([dot(ct[k], l_v[k], NT) for k in range(8)], s2)
    r2[s] = s2[s]
    over_seq(A2, lambda t: s2.at[t], r2)
    gather_second(C1, C2, cf)

    arrived(A2, r2.at[pl.ds(0, NS - 1)])
    fold_src[...] = r2[...].astype(F32)
    for l in range(8):
        m = dot(fold_t, spread(l), NT)
        mon[l] = m
        t = tokp[l].astype(F32)
        go[l // 2, :, 256 * (l % 2) : 256 * (l % 2) + 256] = (t + m * (t * jax.nn.sigmoid(t))).astype(BF16)
    gather_first(G1, G2, go, gf)
    arrived(WZ, w12.at[0, pl.ds(0, 3)])
    send(WC, w12.at[core], w12.at[core], other, c)
    pending.append((WC, w12.at[0]))
    gather_second(G1, G2, gf)

    arrived(WC, w12.at[0])
    eye128 = one_hot((128, 128), lambda a, b: a == b)

    def weight(h, n):
        return w12[:, h, n].reshape(128, 512)

    for h in range(4):
        for n, turned in enumerate((w1t, w2t)):
            held = weight(h, n)
            for b in range(4):
                turned[b, :, 128 * h : 128 * h + 128] = dot(
                    eye128, held[:, 128 * b : 128 * b + 128], NT
                ).astype(BF16)
    arrived(C2, cf.at[pl.ds(0, 12)])
    cot_all = cf[...].reshape(512, 512)
    for h in range(4):
        back[h] = dot(weight(h, 1), cot_all)

    arrived(G2, gf.at[pl.ds(0, 12)])
    gate_all = gf[...].reshape(512, 512)
    for h in range(4):
        value, slope = gelu_parts(dot(weight(h, 0), gate_all))
        hid[h] = value.astype(BF16)
        pg[h] = (back[h] * slope).astype(BF16)

    def partials(weights, units, dst):
        all_units = units[...].reshape(512, 512)
        for b in range(4):
            dst[b] = dot(weights[b], all_units).reshape(4, 32, 512).astype(BF16)

    def total(parts):
        value = parts[0].astype(F32)
        for part in parts[1:]:
            value = value + part.astype(F32)
        return value

    for o in (2, 1, 3, 0):
        to, _ = along_z(o)
        for n, (units, fed) in enumerate(((pg, gate_all), (hid, cot_all))):
            rows = dot(units[to], fed, NT).reshape(16, 8, 512).astype(BF16)
            sg[0, to, 8 * n : 8 * n + 8] = rows[0:8]
            sg[1, to, 8 * n : 8 * n + 8] = rows[8:16]
        send(PC + o, sg.at[1 - core, to], sx.at[to], other, c)
        pending.append((PC + o, sx.at[0]))

    partials(w1t, pg, su)
    for o in (2, 1, 3, 0):
        to, _ = along_z(o)
        for d in (1, 2, 3):
            x = lax.rem(cx + d, 4)
            send(U1 + o, su.at[x, to], ru.at[o, cx], s, 4 * x + cz)
        ru[o, cx] = su[cx, to]
        pending.append((U1 + o, ru.at[0, pl.ds(0, 3)]))

    for o in (2, 1, 3, 0):
        to, _ = along_z(o)
        arrived(PC + o, sx.at[0])
        sp[to] = (sg[core, to].astype(F32) + sx[to].astype(F32)).astype(BF16)

        @pl.loop(1, 16)
        def _(n):
            t = lax.rem(pair + n, 16)
            send(PS, sp.at[to, t], rp.at[pair, to], 2 * t + core, c)

    for z in range(4):
        rp[pair, z] = sp[z, pair]
    pending.append((PS, rp.at[pl.ds(0, 15)]))

    for o in (2, 1, 3, 0):
        to, _ = along_z(o)
        arrived(U1 + o, ru.at[0, pl.ds(0, 3)])
        value = total([ru[o, x] for x in range(4)]).astype(BF16)
        if o == 0:
            ru2[cz] = value
        else:
            su2[o] = value
            send(U2, su2.at[o], ru2.at[cz], s, 4 * cx + to)
    pending.append((U2, ru2.at[pl.ds(0, 3)]))

    partials(w2t, hid, sm)
    for d in (1, 2, 3):
        x = lax.rem(cx + d, 4)
        send(M1, sm.at[x], rm.at[cx], s, 4 * x + cz)
    rm[cx] = sm[cx]
    pending.append((M1, rm.at[pl.ds(0, 3)]))

    arrived(U2, ru2.at[pl.ds(0, 3)])
    rows = []
    for l in range(8):
        at = slice(256 * (l % 2), 256 * (l % 2) + 256)
        t = tokp[l].astype(F32)
        g = cots[l // 2, :, at].astype(F32) + ru2[l // 2, :, at].astype(F32)
        gg[l] = g
        rows.append(g * (t * jax.nn.sigmoid(t)))
    flip(rows, s3)
    r3[s] = s3[s]
    over_seq(A3, lambda t: s3.at[t], r3)

    arrived(M1, rm.at[pl.ds(0, 3)])
    sm2[...] = total([rm[x] for x in range(4)]).astype(BF16)
    rm2[cz] = sm2[cz]
    for o in (2, 1, 3):
        to, _ = along_z(o)
        send(M2, sm2.at[to], rm2.at[cz], s, 4 * cx + to)
    pending.append((M2, rm2.at[pl.ds(0, 3)]))

    arrived(PS, rp.at[pl.ds(0, 15)])
    sq[...] = jnp.sum(rp[...].astype(F32), axis=0).astype(BF16)
    rq[cz] = sq[cz]
    for o in (2, 1, 3):
        to, _ = along_z(o)
        send(PZ, sq.at[to], rq.at[cz], s, 4 * cx + to)
    pending.append((PZ, rq.at[pl.ds(0, 3)]))

    arrived(A3, r3.at[pl.ds(0, NS - 1)])
    fold_src[...] = r3[...].astype(F32)
    flip([dot(dot(fold_t, spread(k), NT).astype(BF16), l_v[k]) for k in range(8)], s4)
    r4[s] = s4[s]
    over_seq(A4, lambda t: s4.at[t], r4)

    arrived(PZ, rq.at[pl.ds(0, 3)])
    sf[...] = total([rq[z] for z in range(4)]).astype(BF16)
    rf[s] = sf[...]
    over_seq(PA, lambda t: sf, rf)

    for k in range(8):
        g = dot(spread(k), fold_t, NT).astype(BF16)
        gl_v[k] = dot(g, ct[k]).astype(BF16)

    arrived(M2, rm2.at[pl.ds(0, 3)])
    for l in range(8):
        at = slice(256 * (l % 2), 256 * (l % 2) + 256)
        value = (go[l // 2, :, at].astype(F32) + rm2[l // 2, :, at].astype(F32)).astype(BF16)
        mixed_v[:, 256 * l : 256 * l + 256] = value[0:GC]
    outs = [pltpu.make_async_copy(gl_v, gl_h, out_sem.at[0]), pltpu.make_async_copy(mixed_v, mixed_h, out_sem.at[1])]
    for copy in outs:
        copy.start()

    arrived(A4, r4.at[pl.ds(0, NS - 1)])
    fold_src[...] = r4[...].astype(F32)
    for i in range(8):
        x = spread(i)
        g = dot(x, fold_t, NT).astype(BF16)
        g_t = dot(fold_t, x, NT).astype(BF16)
        gr_v[i] = dot(g, tokp[i]).astype(BF16)
        t = tokp[i].astype(F32)
        sigma = jax.nn.sigmoid(t)
        through = gg[i] * (1.0 + mon[i] * (sigma * (1.0 + t * (1.0 - sigma))))
        value = (through + dot(g_t, r_v[i])).astype(BF16)
        gin_v[:, 256 * i : 256 * i + 256] = value[0:GC]
    outs += [pltpu.make_async_copy(gr_v, gr_h, out_sem.at[2]), pltpu.make_async_copy(gin_v, gin_h, out_sem.at[3])]
    for copy in outs[2:]:
        copy.start()

    arrived(PA, rf.at[pl.ds(0, NS - 1)])
    halves = rf[...].reshape(16, 2, 8, 512)
    g_in = jnp.concatenate([halves[0:8, k].reshape(64, 512) for k in range(2)], axis=0)
    g_out = jnp.concatenate([halves[8:16, k].reshape(64, 512) for k in range(2)], axis=0)
    gwi_v[...] = dot(pad_cols, g_in, NT)[:, 0:HID].astype(BF16)
    gwo_v[...] = dot(g_out, pad_cols, NT)[0:HID].astype(BF16)
    outs += [pltpu.make_async_copy(gwi_v, gwi_h, out_sem.at[4]), pltpu.make_async_copy(gwo_v, gwo_h, out_sem.at[5])]
    for copy in outs[4:]:
        copy.start()

    for which, view in pending:
        sent(which, view)
    for copy in outs:
        copy.wait()


def hand_over(*refs):
    held, into, out = refs[12:18], refs[18], refs[19]
    reads = [pltpu.make_async_copy(refs[m], held[m], into.at[m]) for m in range(6)]
    writes = [pltpu.make_async_copy(held[m], refs[6 + m], out.at[m]) for m in range(6)]
    for copy in reads:
        copy.start()
    for read, write in zip(reads, writes):
        read.wait()
        write.start()
    for copy in writes:
        copy.wait()


def local(tokens, cotangent, right_blocks, left_blocks, w_in, w_out):
    piece = (NS, 8, 256)
    scratch = [
        ((GC, 2048), BF16), ((GC, 2048), BF16), ((8, 256, 256), BF16), ((8, 256, 256), BF16),
        ((480, HID), BF16), ((HID, 480), BF16),
        ((8, 32, 256), BF16), ((4, 32, 512), BF16),
        (piece, BF16), (piece, BF16), (piece, BF16), (piece, BF16),
        (piece, BF16), (piece, BF16), (piece, BF16), (piece, BF16),
        (piece, F32), ((8, 32, 256), BF16), ((8, 32, 256), F32),
        ((4, 32, 512), BF16), ((16, 32, 512), BF16), ((16, 32, 512), BF16),
        ((2, 2, 64, 512), BF16), ((2, 4, 2, 64, 512), BF16),
        ((4, 128, 512), BF16), ((4, 128, 512), BF16), ((4, 128, 512), F32),
        ((4, 128, 512), BF16), ((4, 128, 512), BF16),
        ((4, 4, 32, 512), BF16), ((4, 4, 32, 512), BF16), ((4, 32, 512), BF16), ((4, 32, 512), BF16),
        ((4, 4, 32, 512), BF16), ((4, 4, 32, 512), BF16), ((4, 32, 512), BF16), ((4, 32, 512), BF16),
        ((2, 4, 16, 8, 512), BF16), ((4, 16, 8, 512), BF16), ((4, 16, 8, 512), BF16), ((16, 4, 8, 512), BF16),
        ((4, 8, 512), BF16), ((4, 8, 512), BF16), ((8, 512), BF16), ((NS, 8, 512), BF16),
        ((8, 32, 256), F32),
        ((GC, 2048), BF16), ((GC, 2048), BF16), ((8, 256, 256), BF16), ((8, 256, 256), BF16),
        ((480, HID), BF16), ((HID, 480), BF16),
    ]
    shapes = [
        ((GC, 2048), BF16), ((GC, 2048), BF16), ((8, 256, 256), BF16), ((8, 256, 256), BF16),
        ((480, HID), BF16), ((HID, 480), BF16),
    ]
    results = pl.pallas_call(
        kernel,
        out_shape=[jax.ShapeDtypeStruct(*shape) for shape in shapes],
        in_specs=[pl.BlockSpec(memory_space=pl.ANY)] * 6,
        out_specs=[pl.BlockSpec(memory_space=pl.ANY)] * 6,
        scratch_shapes=[pltpu.VMEM(*shape) for shape in scratch]
        + [pltpu.SemaphoreType.DMA((6,)), pltpu.SemaphoreType.DMA((6,))]
        + [pltpu.SemaphoreType.DMA((N_SEM,)), pltpu.SemaphoreType.DMA((N_SEM,))],
        compiler_params=pltpu.CompilerParams(
            collective_id=0, has_side_effects=True, vmem_limit_bytes=VMEM_LIMIT
        ),
        name="monarch_block",
    )(tokens, cotangent, right_blocks[0], left_blocks[0], w_in, w_out)
    mixed, gin, gr, gl, gwi, gwo = pl.pallas_call(
        hand_over,
        out_shape=[jax.ShapeDtypeStruct(*shape) for shape in shapes],
        in_specs=[pl.BlockSpec(memory_space=pl.ANY)] * 6,
        out_specs=[pl.BlockSpec(memory_space=pl.ANY)] * 6,
        scratch_shapes=[pltpu.VMEM(*shape) for shape in shapes] + [pltpu.SemaphoreType.DMA((6,))] * 2,
        compiler_params=pltpu.CompilerParams(vmem_limit_bytes=VMEM_LIMIT),
        name="hand_over",
    )(*results)
    return mixed, gin, gr[None], gl[None], gwi, gwo


def solution(mesh):
    placed = (
        P("ch", "seq"),
        P("ch", "seq"),
        P("ch", "seq", None, None),
        P("ch", "seq", None, None),
        P(None, "ch"),
        P("ch", None),
    )
    return jax.shard_map(
        local,
        mesh=mesh,
        in_specs=placed,
        out_specs=placed,
        check_vma=False,
    )
```

```python
import jax
import jax.numpy as jnp
from jax import lax
from jax.experimental import pallas as pl
from jax.experimental.pallas import tpu as pltpu
from jax.sharding import PartitionSpec as P

NS = 32
NC = 16
GC = 30
HID = 120
VMEM_LIMIT = 60 * 1024 * 1024
F32 = jnp.float32
BF16 = jnp.bfloat16
MESH = pl.DeviceIdType.MESH

NN = (((1,), (0,)), ((), ()))
NT = (((1,), (1,)), ((), ()))
TN = (((0,), (0,)), ((), ()))

A1, A2, A3, A4 = 0, 1, 2, 3
C1, C2, G1, G2 = 4, 8, 9, 13
WZ, WC = 14, 15
U1, U2, M1, M2 = 16, 20, 21, 22
PC, PS, PZ, PA = 23, 27, 28, 29
N_SEM = 30


def dot(a, b, dims=NN):
    return lax.dot_general(a, b, dims, preferred_element_type=F32)


def one_hot(shape, test):
    rows = lax.broadcasted_iota(jnp.int32, shape, 0)
    cols = lax.broadcasted_iota(jnp.int32, shape, 1)
    return jnp.where(test(rows, cols), 1.0, 0.0).astype(BF16)


def gelu_parts(v):
    cdf = 0.5 * (1.0 + lax.erf(v * 0.7071067811865476))
    return v * cdf, cdf + v * jnp.exp(-0.5 * v * v) * 0.3989422804014327


def kernel(
    tok_h, cot_h, r_h, l_h, wi_h, wo_h,
    mixed_h, gin_h, gr_h, gl_h, gwi_h, gwo_h,
    tok_v, cot_v, r_v, l_v, wi_v, wo_v,
    tokp, cots, s1, r1, s2, r2, s3, r3, s4, r4,
    fold_src, ct, mon, go, gf, cf, ws, w12, w1t, w2t, back, hid, pg,
    su, ru, su2, ru2, sm, rm, sm2, rm2,
    sg, sx, sp, rp, sq, rq, sf, rf, gg,
    mixed_v, gin_v, gl_v, gr_v, gwi_v, gwo_v,
    in_sem, out_sem, send_sem, recv_sem,
):
    s, c = lax.axis_index("seq"), lax.axis_index("ch")
    cx, cz = c // 4, lax.rem(c, 4)
    core = lax.rem(s, 2)
    pair = s // 2
    other = s + 1 - 2 * core

    barrier = pltpu.get_barrier_semaphore()

    @pl.loop(1, NS)
    def _(o):
        pl.semaphore_signal(barrier, inc=1, device_id={"seq": lax.rem(s + o, NS), "ch": c}, device_id_type=MESH)

    @pl.loop(1, NC)
    def _(o):
        pl.semaphore_signal(barrier, inc=1, device_id={"seq": s, "ch": lax.rem(c + o, NC)}, device_id_type=MESH)

    ins = [
        pltpu.make_async_copy(src, dst, in_sem.at[n])
        for n, (src, dst) in enumerate(
            ((tok_h, tok_v), (r_h, r_v), (cot_h, cot_v), (wi_h, wi_v), (wo_h, wo_v), (l_h, l_v))
        )
    ]
    for copy in ins:
        copy.start()

    pending = []

    def send(which, src, dst, seq, ch):
        pltpu.make_async_remote_copy(
            src_ref=src, dst_ref=dst, send_sem=send_sem.at[which], recv_sem=recv_sem.at[which],
            device_id={"seq": seq, "ch": ch}, device_id_type=MESH,
        ).start()

    def over_seq(which, src_of, dst):
        @pl.loop(1, NS)
        def _(o):
            t = lax.rem(s + o, NS)
            send(which, src_of(t), dst.at[s], t, c)

        pending.append((which, dst.at[pl.ds(0, NS - 1)]))

    def along_x(which, src, dst):
        for o in (1, 2, 3):
            send(which, src, dst, s, lax.rem(cx + o, 4) * 4 + cz)

    def along_z(o):
        return lax.rem(cz + o, 4), lax.rem(cz + 4 - o, 4)

    def arrived(which, view):
        pltpu.make_async_copy(view, view, recv_sem.at[which]).wait()

    def sent(which, view):
        pltpu.make_async_copy(view, view, send_sem.at[which]).wait()

    def gather_first(z_sem, x_sem, src, dst):
        for o in (2, 1, 3):
            to, _ = along_z(o)
            send(z_sem + o, src.at[to], dst.at[c], s, 4 * cx + to)
            pending.append((z_sem + o, dst.at[0]))
        dst[c] = src[cz]
        along_x(x_sem, src.at[cz], dst.at[c])

    def gather_second(z_sem, x_sem, dst):
        for o in (1, 3, 2):
            _, frm = along_z(o)
            arrived(z_sem + o, dst.at[0])
            along_x(x_sem, dst.at[4 * cx + frm], dst.at[4 * cx + frm])
        pending.append((x_sem, dst.at[pl.ds(0, 12)]))

    eye = one_hot((256, 256), lambda a, b: a == b)
    fold_t = one_hot((32, 256), lambda a, b: a == (b & 31))
    keep = (
        (lax.broadcasted_iota(jnp.int32, (8, 256), 1) >> 5) == lax.broadcasted_iota(jnp.int32, (8, 256), 0)
    )[None]

    def spread(n):
        row = jnp.broadcast_to(fold_src[:, n : n + 1, :], (NS, 8, 256))
        return jnp.where(keep, row, 0.0).reshape(256, 256).astype(BF16)

    def flip(rows, dst):
        stacked = jnp.concatenate([row.astype(BF16) for row in rows], axis=0)
        dst[...] = dot(eye, stacked, NT).reshape(NS, 8, 256).astype(BF16)

    ins[0].wait()
    tokp[...] = jnp.zeros_like(tokp)
    for i in range(8):
        tokp[i, 0:GC, :] = tok_v[:, 256 * i : 256 * i + 256]
    ins[1].wait()
    flip([dot(tokp[i], r_v[i], NT) for i in range(8)], s1)
    r1[s] = s1[s]
    pl.semaphore_wait(barrier, NS + NC - 2)
    over_seq(A1, lambda t: s1.at[t], r1)

    ins[2].wait()
    cots[...] = jnp.zeros_like(cots)
    for q in range(4):
        cots[q, 0:GC, :] = cot_v[:, 512 * q : 512 * q + 512]
    gather_first(C1, C2, cots, cf)
    pad_cols = one_hot(
        (GC * NC, 512), lambda a, b: (a == GC * (b >> 5) + (b & 31)) & ((b & 31) < GC)
    )
    ins[3].wait()
    ins[4].wait()
    for n, rows in enumerate((dot(wi_v[...], pad_cols, TN), dot(wo_v[...], pad_cols))):
        ws[0, n] = rows[0:64].astype(BF16)
        ws[1, n] = jnp.zeros((64, 512), BF16)
        ws[1, n, 0 : HID - 64, :] = rows[64:HID].astype(BF16)
    w12[core, cz] = ws[core]
    for o in (1, 2, 3):
        to, _ = along_z(o)
        send(WZ, ws.at[core], w12.at[core, cz], s, 4 * cx + to)
    pending.append((WZ, w12.at[0, pl.ds(0, 3)]))

    ins[5].wait()
    arrived(A1, r1.at[pl.ds(0, NS - 1)])
    fold_src[...] = r1[...].astype(F32)
    for k in range(8):
        ct[k] = dot(fold_t, spread(k), NT).astype(BF16)
    flip([dot(ct[k], l_v[k], NT) for k in range(8)], s2)
    r2[s] = s2[s]
    over_seq(A2, lambda t: s2.at[t], r2)
    gather_second(C1, C2, cf)

    arrived(A2, r2.at[pl.ds(0, NS - 1)])
    fold_src[...] = r2[...].astype(F32)
    for l in range(8):
        m = dot(fold_t, spread(l), NT)
        mon[l] = m
        t = tokp[l].astype(F32)
        go[l // 2, :, 256 * (l % 2) : 256 * (l % 2) + 256] = (t + m * (t * jax.nn.sigmoid(t))).astype(BF16)
    gather_first(G1, G2, go, gf)
    arrived(WZ, w12.at[0, pl.ds(0, 3)])
    send(WC, w12.at[core], w12.at[core], other, c)
    pending.append((WC, w12.at[0]))
    gather_second(G1, G2, gf)

    arrived(WC, w12.at[0])
    eye128 = one_hot((128, 128), lambda a, b: a == b)

    def weight(h, n):
        return w12[:, h, n].reshape(128, 512)

    for h in range(4):
        for n, turned in enumerate((w1t, w2t)):
            held = weight(h, n)
            for b in range(4):
                turned[b, :, 128 * h : 128 * h + 128] = dot(
                    eye128, held[:, 128 * b : 128 * b + 128], NT
                ).astype(BF16)
    arrived(C2, cf.at[pl.ds(0, 12)])
    cot_all = cf[...].reshape(512, 512)
    for h in range(4):
        back[h] = dot(weight(h, 1), cot_all)

    arrived(G2, gf.at[pl.ds(0, 12)])
    gate_all = gf[...].reshape(512, 512)
    for h in range(4):
        value, slope = gelu_parts(dot(weight(h, 0), gate_all))
        hid[h] = value.astype(BF16)
        pg[h] = (back[h] * slope).astype(BF16)

    def partials(weights, units, dst):
        all_units = units[...].reshape(512, 512)
        for b in range(4):
            dst[b] = dot(weights[b], all_units).reshape(4, 32, 512).astype(BF16)

    def total(parts):
        value = parts[0].astype(F32)
        for part in parts[1:]:
            value = value + part.astype(F32)
        return value

    for o in (2, 1, 3, 0):
        to, _ = along_z(o)
        for n, (units, fed) in enumerate(((pg, gate_all), (hid, cot_all))):
            rows = dot(units[to], fed, NT).reshape(16, 8, 512).astype(BF16)
            sg[0, to, 8 * n : 8 * n + 8] = rows[0:8]
            sg[1, to, 8 * n : 8 * n + 8] = rows[8:16]
        send(PC + o, sg.at[1 - core, to], sx.at[to], other, c)
        pending.append((PC + o, sx.at[0]))

    partials(w1t, pg, su)
    for o in (2, 1, 3, 0):
        to, _ = along_z(o)
        for d in (1, 2, 3):
            x = lax.rem(cx + d, 4)
            send(U1 + o, su.at[x, to], ru.at[o, cx], s, 4 * x + cz)
        ru[o, cx] = su[cx, to]
        pending.append((U1 + o, ru.at[0, pl.ds(0, 3)]))

    for o in (2, 1, 3, 0):
        to, _ = along_z(o)
        arrived(PC + o, sx.at[0])
        sp[to] = (sg[core, to].astype(F32) + sx[to].astype(F32)).astype(BF16)

        @pl.loop(1, 16)
        def _(n):
            t = lax.rem(pair + n, 16)
            send(PS, sp.at[to, t], rp.at[pair, to], 2 * t + core, c)

    for z in range(4):
        rp[pair, z] = sp[z, pair]
    pending.append((PS, rp.at[pl.ds(0, 15)]))

    for o in (2, 1, 3, 0):
        to, _ = along_z(o)
        arrived(U1 + o, ru.at[0, pl.ds(0, 3)])
        value = total([ru[o, x] for x in range(4)]).astype(BF16)
        if o == 0:
            ru2[cz] = value
        else:
            su2[o] = value
            send(U2, su2.at[o], ru2.at[cz], s, 4 * cx + to)
    pending.append((U2, ru2.at[pl.ds(0, 3)]))

    partials(w2t, hid, sm)
    for d in (1, 2, 3):
        x = lax.rem(cx + d, 4)
        send(M1, sm.at[x], rm.at[cx], s, 4 * x + cz)
    rm[cx] = sm[cx]
    pending.append((M1, rm.at[pl.ds(0, 3)]))

    arrived(U2, ru2.at[pl.ds(0, 3)])
    rows = []
    for l in range(8):
        at = slice(256 * (l % 2), 256 * (l % 2) + 256)
        t = tokp[l].astype(F32)
        g = cots[l // 2, :, at].astype(F32) + ru2[l // 2, :, at].astype(F32)
        gg[l] = g
        rows.append(g * (t * jax.nn.sigmoid(t)))
    flip(rows, s3)
    r3[s] = s3[s]
    over_seq(A3, lambda t: s3.at[t], r3)

    arrived(M1, rm.at[pl.ds(0, 3)])
    sm2[...] = total([rm[x] for x in range(4)]).astype(BF16)
    rm2[cz] = sm2[cz]
    for o in (2, 1, 3):
        to, _ = along_z(o)
        send(M2, sm2.at[to], rm2.at[cz], s, 4 * cx + to)
    pending.append((M2, rm2.at[pl.ds(0, 3)]))

    arrived(PS, rp.at[pl.ds(0, 15)])
    sq[...] = jnp.sum(rp[...].astype(F32), axis=0).astype(BF16)
    rq[cz] = sq[cz]
    for o in (2, 1, 3):
        to, _ = along_z(o)
        send(PZ, sq.at[to], rq.at[cz], s, 4 * cx + to)
    pending.append((PZ, rq.at[pl.ds(0, 3)]))

    arrived(A3, r3.at[pl.ds(0, NS - 1)])
    fold_src[...] = r3[...].astype(F32)
    flip([dot(dot(fold_t, spread(k), NT).astype(BF16), l_v[k]) for k in range(8)], s4)
    r4[s] = s4[s]
    over_seq(A4, lambda t: s4.at[t], r4)

    arrived(PZ, rq.at[pl.ds(0, 3)])
    sf[...] = total([rq[z] for z in range(4)]).astype(BF16)
    rf[s] = sf[...]
    over_seq(PA, lambda t: sf, rf)

    for k in range(8):
        g = dot(spread(k), fold_t, NT).astype(BF16)
        gl_v[k] = dot(g, ct[k]).astype(BF16)

    arrived(M2, rm2.at[pl.ds(0, 3)])
    for l in range(8):
        at = slice(256 * (l % 2), 256 * (l % 2) + 256)
        value = (go[l // 2, :, at].astype(F32) + rm2[l // 2, :, at].astype(F32)).astype(BF16)
        mixed_v[:, 256 * l : 256 * l + 256] = value[0:GC]
    outs = [pltpu.make_async_copy(gl_v, gl_h, out_sem.at[0]), pltpu.make_async_copy(mixed_v, mixed_h, out_sem.at[1])]
    for copy in outs:
        copy.start()

    arrived(A4, r4.at[pl.ds(0, NS - 1)])
    fold_src[...] = r4[...].astype(F32)
    for i in range(8):
        x = spread(i)
        g = dot(x, fold_t, NT).astype(BF16)
        g_t = dot(fold_t, x, NT).astype(BF16)
        gr_v[i] = dot(g, tokp[i]).astype(BF16)
        t = tokp[i].astype(F32)
        sigma = jax.nn.sigmoid(t)
        through = gg[i] * (1.0 + mon[i] * (sigma * (1.0 + t * (1.0 - sigma))))
        value = (through + dot(g_t, r_v[i])).astype(BF16)
        gin_v[:, 256 * i : 256 * i + 256] = value[0:GC]
    outs += [pltpu.make_async_copy(gr_v, gr_h, out_sem.at[2]), pltpu.make_async_copy(gin_v, gin_h, out_sem.at[3])]
    for copy in outs[2:]:
        copy.start()

    arrived(PA, rf.at[pl.ds(0, NS - 1)])
    halves = rf[...].reshape(16, 2, 8, 512)
    g_in = jnp.concatenate([halves[0:8, k].reshape(64, 512) for k in range(2)], axis=0)
    g_out = jnp.concatenate([halves[8:16, k].reshape(64, 512) for k in range(2)], axis=0)
    gwi_v[...] = dot(pad_cols, g_in, NT)[:, 0:HID].astype(BF16)
    gwo_v[...] = dot(g_out, pad_cols, NT)[0:HID].astype(BF16)
    outs += [pltpu.make_async_copy(gwi_v, gwi_h, out_sem.at[4]), pltpu.make_async_copy(gwo_v, gwo_h, out_sem.at[5])]
    for copy in outs[4:]:
        copy.start()

    for which, view in pending:
        sent(which, view)
    for copy in outs:
        copy.wait()


def hand_over(*refs):
    held, into, out = refs[12:18], refs[18], refs[19]
    parts = [(m, slice(None)) for m in (0, 1, 4, 5)]
    parts = [(m, pl.ds(2 * n, 2)) for n in range(4) for m in (2, 3)] + parts
    reads = [
        pltpu.make_async_copy(refs[m].at[at], held[m].at[at], into.at[n]) for n, (m, at) in enumerate(parts)
    ]
    writes = [
        pltpu.make_async_copy(held[m].at[at], refs[6 + m].at[at], out.at[n]) for n, (m, at) in enumerate(parts)
    ]
    for copy in reads:
        copy.start()
    for read, write in zip(reads, writes):
        read.wait()
        write.start()
    for copy in writes:
        copy.wait()


def local(tokens, cotangent, right_blocks, left_blocks, w_in, w_out):
    piece = (NS, 8, 256)
    scratch = [
        ((GC, 2048), BF16), ((GC, 2048), BF16), ((8, 256, 256), BF16), ((8, 256, 256), BF16),
        ((480, HID), BF16), ((HID, 480), BF16),
        ((8, 32, 256), BF16), ((4, 32, 512), BF16),
        (piece, BF16), (piece, BF16), (piece, BF16), (piece, BF16),
        (piece, BF16), (piece, BF16), (piece, BF16), (piece, BF16),
        (piece, F32), ((8, 32, 256), BF16), ((8, 32, 256), F32),
        ((4, 32, 512), BF16), ((16, 32, 512), BF16), ((16, 32, 512), BF16),
        ((2, 2, 64, 512), BF16), ((2, 4, 2, 64, 512), BF16),
        ((4, 128, 512), BF16), ((4, 128, 512), BF16), ((4, 128, 512), F32),
        ((4, 128, 512), BF16), ((4, 128, 512), BF16),
        ((4, 4, 32, 512), BF16), ((4, 4, 32, 512), BF16), ((4, 32, 512), BF16), ((4, 32, 512), BF16),
        ((4, 4, 32, 512), BF16), ((4, 4, 32, 512), BF16), ((4, 32, 512), BF16), ((4, 32, 512), BF16),
        ((2, 4, 16, 8, 512), BF16), ((4, 16, 8, 512), BF16), ((4, 16, 8, 512), BF16), ((16, 4, 8, 512), BF16),
        ((4, 8, 512), BF16), ((4, 8, 512), BF16), ((8, 512), BF16), ((NS, 8, 512), BF16),
        ((8, 32, 256), F32),
        ((GC, 2048), BF16), ((GC, 2048), BF16), ((8, 256, 256), BF16), ((8, 256, 256), BF16),
        ((480, HID), BF16), ((HID, 480), BF16),
    ]
    shapes = [
        ((GC, 2048), BF16), ((GC, 2048), BF16), ((8, 256, 256), BF16), ((8, 256, 256), BF16),
        ((480, HID), BF16), ((HID, 480), BF16),
    ]
    results = pl.pallas_call(
        kernel,
        out_shape=[jax.ShapeDtypeStruct(*shape) for shape in shapes],
        in_specs=[pl.BlockSpec(memory_space=pl.ANY)] * 6,
        out_specs=[pl.BlockSpec(memory_space=pl.ANY)] * 6,
        scratch_shapes=[pltpu.VMEM(*shape) for shape in scratch]
        + [pltpu.SemaphoreType.DMA((6,)), pltpu.SemaphoreType.DMA((6,))]
        + [pltpu.SemaphoreType.DMA((N_SEM,)), pltpu.SemaphoreType.DMA((N_SEM,))],
        compiler_params=pltpu.CompilerParams(
            collective_id=0, has_side_effects=True, vmem_limit_bytes=VMEM_LIMIT
        ),
        name="monarch_block",
    )(tokens, cotangent, right_blocks[0], left_blocks[0], w_in, w_out)
    mixed, gin, gr, gl, gwi, gwo = pl.pallas_call(
        hand_over,
        out_shape=[jax.ShapeDtypeStruct(*shape) for shape in shapes],
        in_specs=[pl.BlockSpec(memory_space=pl.ANY)] * 6,
        out_specs=[pl.BlockSpec(memory_space=pl.ANY)] * 6,
        scratch_shapes=[pltpu.VMEM(*shape) for shape in shapes] + [pltpu.SemaphoreType.DMA((12,))] * 2,
        compiler_params=pltpu.CompilerParams(vmem_limit_bytes=VMEM_LIMIT),
        name="hand_over",
    )(*results)
    return mixed, gin, gr[None], gl[None], gwi, gwo


def solution(mesh):
    placed = (
        P("ch", "seq"),
        P("ch", "seq"),
        P("ch", "seq", None, None),
        P("ch", "seq", None, None),
        P(None, "ch"),
        P("ch", None),
    )
    return jax.shard_map(
        local,
        mesh=mesh,
        in_specs=placed,
        out_specs=placed,
        check_vma=False,
    )
```
